32 devices in a mesh: flow: 4 (over z), cross: 8 (over y, x, core).
Axes of the slice: x: 2, y: 2, z: 4, core: 2. Of those that a mesh axis runs over, the one named last changes fastest.
Arguments:
- rhs: bfloat16 [4, 8, 16, 32, 1024], P('flow', 'cross'), may hold values from -6 to 6
- inverses: bfloat16 [4, 8, 16, 16, 1024], P('flow', 'cross'), as said below
- flux_weights: float32 [4, 8, 4, 1024], P('flow', 'cross'), may hold values from 0.05 to 0.4
- upwind_index: int32 [4, 8, 4, 1024], P('flow', 'cross'), may hold values from 0 to 1279, as said below
- sweep_order: int32 [4, 8, 1024], P('flow', 'cross'), may hold values from 0 to 1023, each once within a row
- level_counts: int32 [4, 8, 8], P('flow', 'cross'), may hold values from 32 to 128, as said below
- boundary_traces: float32 [4, 16, 3, 32, 128], P('flow', 'cross'), may hold values from -6 to 6
- trace_map: float32 [3, 16], replicated, may hold values from -0.42 to 0.42
- lift_map: float32 [16, 3], replicated, may hold values from -1.4 to 1.4
Outputs:
- solution: float32 [4, 8, 16, 32, 1024], P('flow', 'cross')
The draws below stay inside these ranges and needn't reach their ends.
Inputs may be any that keep to these rules, and one draw needn't show every extreme that they name: `upwind_index`: an entry of a slot of level l is below 384 + l * 128: it names an inflow trace, a cross-stream rim trace or an own slot of an earlier level. Face 1 of every slot and face 0 of every slot of level 0 name inflow traces. `level_counts`: level 0 of every partition is full. `inverses`: each entry is a cell block's inverse, with unit-order diagonal.
All inputs are finite; a program needn't handle non-finite values.
Results may differ from the reference program's by a relative error of at most 0.0003.
Values sent between devices are 32-bit elements; how exact they have to be, the bound alone decides.
No kernel may reach another device: no remote copies, remote signals or barrier semaphores. Data moves between devices by JAX's collectives and lax.ppermute only.
A program may use at most 64 MiB of HBM per device.

```python
import jax
import jax.numpy as jnp
from jax import lax

TRACERS = 32
BLOCK = 16
FACE_DOFS = 3
FACES = 4
LEVELS = 8
LEVEL_CELLS = 128
RIM = 128
CELLS = 1024
FLOWS = 4
COLUMNS = 8


lift_scale = 1.0


trace_scale = 0.3


def draw_upwind_index(key, part):
    shape = (FLOWS, COLUMNS, CELLS)
    level_of = jnp.arange(CELLS, dtype=jnp.int32) // LEVEL_CELLS
    own_start = LEVEL_CELLS + 2 * RIM
    keys = jax.random.split(jax.random.fold_in(key, 11), 6)
    inflow_one = jax.random.randint(keys[0], shape, 0, LEVEL_CELLS)
    inflow_two = jax.random.randint(keys[1], shape, 0, LEVEL_CELLS)
    previous = own_start + (level_of - 1) * LEVEL_CELLS + jax.random.randint(keys[2], shape, 0, LEVEL_CELLS)
    face_zero = jnp.where(level_of == 0, inflow_one, previous)
    face_one = inflow_two
    face_two = LEVEL_CELLS + jax.random.randint(keys[4], shape, 0, 2 * RIM)
    rest = jax.random.randint(keys[5], (FLOWS, COLUMNS, FACES - 3, CELLS), 0, own_start + level_of * LEVEL_CELLS)
    result = jnp.concatenate([face_zero[:, :, None], face_one[:, :, None], face_two[:, :, None], rest], axis=2)
    result = result.at[:, :, 0, 0].set(0)
    result = result.at[:, :, FACES - 1, CELLS - 1].set(2 * RIM + CELLS - 1)
    return result.astype(jnp.int32)


def draw_level_counts(key, part):
    counts = jax.random.randint(jax.random.fold_in(key, 23), (FLOWS, COLUMNS, LEVELS), LEVEL_CELLS // 4, LEVEL_CELLS + 1)
    counts = counts.at[:, :, 0].set(LEVEL_CELLS)
    counts = counts.at[0, 0, LEVELS - 1].set(LEVEL_CELLS // 4)
    return counts.astype(jnp.int32)


def draw_inverses(key, part):
    shape = (FLOWS, COLUMNS, BLOCK, BLOCK, CELLS)
    key_diag, key_off = jax.random.split(jax.random.fold_in(key, 37))
    identity = jnp.eye(BLOCK, dtype=jnp.float32)[:, :, None]
    diagonal = jax.random.uniform(key_diag, shape, jnp.float32, 0.5, 1.0)
    off_part = 0.1 * jax.random.normal(key_off, shape, jnp.float32)
    result = identity * diagonal + (1.0 - identity) * off_part
    return result.astype(jnp.bfloat16)


def draw_rhs(key, part):
    shape = (FLOWS, COLUMNS, BLOCK, TRACERS, CELLS)
    key_rough = jax.random.fold_in(jax.random.fold_in(key, 41), 0)
    result = jnp.clip(jax.random.normal(key_rough, shape, jnp.float32), -6.0, 6.0)
    return result.astype(jnp.bfloat16)


def draw_flux_weights(key, part):
    shape = (FLOWS, COLUMNS, FACES, CELLS)
    key_near, key_far = jax.random.split(jax.random.fold_in(key, 43))
    face_ids = jnp.arange(FACES, dtype=jnp.int32)[None, None, :, None]
    near = jnp.exp(jax.random.uniform(key_near, shape, jnp.float32, jnp.log(0.15), jnp.log(0.4)))
    far = jnp.exp(jax.random.uniform(key_far, shape, jnp.float32, jnp.log(0.05), jnp.log(0.4)))
    result = jnp.where(face_ids < 2, near, far)
    return jnp.clip(result, 0.05, 0.4).astype(jnp.float32)


def aligned_pattern(key):
    flips = jax.random.uniform(jax.random.fold_in(key, 51), (BLOCK, FACE_DOFS), jnp.float32)
    sign_flip = jnp.where(flips < 0.5, -1.0, 1.0)
    home_mask = jnp.arange(BLOCK)[:, None] % FACE_DOFS == jnp.arange(FACE_DOFS)[None, :]
    reach = jnp.where(home_mask, 1.0, 0.25)
    return sign_flip * reach


def draw_lift_map(key, part):
    pattern = aligned_pattern(key)
    magnitude = jax.random.uniform(jax.random.fold_in(key, 53), (BLOCK, FACE_DOFS), jnp.float32, 0.6, 1.4)
    return (lift_scale * pattern * magnitude).astype(jnp.float32)


def draw_trace_map(key, part):
    pattern = aligned_pattern(key)
    magnitude = jax.random.uniform(jax.random.fold_in(key, 59), (BLOCK, FACE_DOFS), jnp.float32, 0.6, 1.4)
    return (trace_scale * pattern * magnitude).T.astype(jnp.float32)


def steps_of(own_key, extent, shards, low, largest):
    def one(position, blocks):
        steps = jax.random.uniform(jax.random.fold_in(jax.random.fold_in(own_key, 6), position), (blocks,), jnp.float32, low / len(shards), largest / len(shards))
        return jnp.repeat(jnp.exp(steps), extent[position] // blocks).reshape((-1,) + (1,) * (len(extent) - position - 1))

    gain = one(*shards[0])
    for cut in shards[1:]:
        gain = gain * one(*cut)
    return gain


def normal_values(rng, dims, scale, bound, cuts=(), held_as=jnp.bfloat16):
    values = jax.random.normal(rng, dims, jnp.float32) * scale
    if len(cuts) > 0:
        values = steps_of(rng, dims, cuts, -0.22, 0.18) * values
    return jnp.clip(values, min=-bound, max=bound).astype(held_as)


def setup_inputs(seed: int = 0) -> dict:
    seeds = jax.random.split(jax.random.key(seed), 10)
    rhs = draw_rhs(jax.random.fold_in(seeds[9], 71), 0)
    inverses = draw_inverses(jax.random.fold_in(seeds[9], 71), 0)
    flux_weights = draw_flux_weights(jax.random.fold_in(seeds[9], 71), 0)
    upwind_index = draw_upwind_index(jax.random.fold_in(seeds[9], 71), 0)
    sweep_order = jax.vmap(lambda own: jax.random.permutation(own, CELLS))(jax.random.split(seeds[4], FLOWS * COLUMNS)).reshape((FLOWS, COLUMNS, CELLS)).astype(jnp.int32)
    level_counts = draw_level_counts(jax.random.fold_in(seeds[9], 71), 0)
    boundary_traces = normal_values(seeds[6], (FLOWS, 2 * COLUMNS, FACE_DOFS, TRACERS, RIM), 1.0, 6.0, ((0, 4), (1, 8)), jnp.float32)
    trace_map = draw_trace_map(jax.random.fold_in(seeds[9], 71), 0)
    lift_map = draw_lift_map(jax.random.fold_in(seeds[9], 71), 0)
    return dict(rhs=rhs, inverses=inverses, flux_weights=flux_weights, upwind_index=upwind_index, sweep_order=sweep_order, level_counts=level_counts, boundary_traces=boundary_traces, trace_map=trace_map, lift_map=lift_map)


def sweep_partition(rhs_part, inv_part, weights_part, index_part, order_part, counts_part, inflow, rim_pool, trace_map, lift_map):
    level_rhs = rhs_part[:, :, order_part].astype(jnp.float32)
    level_inv = inv_part[:, :, order_part].astype(jnp.float32)
    own_start = LEVEL_CELLS + 2 * RIM
    source_pool = jnp.concatenate([inflow, rim_pool, jnp.zeros((FACE_DOFS, TRACERS, CELLS), jnp.float32)], axis=2)
    slot_ids = jnp.arange(LEVEL_CELLS, dtype=jnp.int32)
    solved_levels = []
    traces = inflow
    for sweep_level in range(LEVELS):
        offset = sweep_level * LEVEL_CELLS
        faces_at = index_part[:, offset:offset + LEVEL_CELLS]
        weights_at = weights_part[:, offset:offset + LEVEL_CELLS]
        upwind_vals = source_pool[:, :, faces_at]
        carried = jnp.sum(upwind_vals * weights_at[None, None], axis=2)
        lifted = jnp.einsum("af,ftc->atc", lift_map, carried, precision=lax.Precision.HIGHEST)
        totals = level_rhs[:, :, offset:offset + LEVEL_CELLS] + lifted
        solved = jnp.einsum("abc,btc->atc", level_inv[:, :, offset:offset + LEVEL_CELLS], totals, precision=lax.Precision.HIGHEST)
        alive_mask = (slot_ids < counts_part[sweep_level]).astype(jnp.float32)
        solved = solved * alive_mask
        traces = jnp.einsum("fa,atc->ftc", trace_map, solved, precision=lax.Precision.HIGHEST)
        source_pool = source_pool.at[:, :, own_start + offset:own_start + offset + LEVEL_CELLS].set(traces)
        solved_levels.append(solved)
    level_solution = jnp.concatenate(solved_levels, axis=2)
    stored = jnp.zeros((BLOCK, TRACERS, CELLS), jnp.float32).at[:, :, order_part].set(level_solution)
    return stored, traces


def reference(rhs, inverses, flux_weights, upwind_index, sweep_order, level_counts, boundary_traces, trace_map, lift_map):
    rows = boundary_traces.reshape(FLOWS, COLUMNS, 2, FACE_DOFS, TRACERS, RIM)
    empty_rim = jnp.zeros((1, FACE_DOFS, TRACERS, RIM), jnp.float32)
    inflow = jnp.zeros((COLUMNS, FACE_DOFS, TRACERS, LEVEL_CELLS), jnp.float32)
    sweep_all = jax.vmap(sweep_partition, in_axes=(0, 0, 0, 0, 0, 0, 0, 0, None, None))
    results = []
    for flow_pos in range(FLOWS):
        lower_side = jnp.concatenate([empty_rim, rows[flow_pos, :-1, 1]], axis=0)
        upper_side = jnp.concatenate([rows[flow_pos, 1:, 0], empty_rim], axis=0)
        rim_pool = jnp.concatenate([lower_side, upper_side], axis=3)
        stored, inflow = sweep_all(rhs[flow_pos], inverses[flow_pos], flux_weights[flow_pos], upwind_index[flow_pos], sweep_order[flow_pos], level_counts[flow_pos], inflow, rim_pool, trace_map, lift_map)
        results.append(stored)
    return jnp.stack(results, axis=0)
```

```python
import functools

import jax
import jax.numpy as jnp
from jax import lax
from jax.experimental import pallas as pl
from jax.experimental.pallas import tpu as pltpu
from jax.sharding import PartitionSpec as P

F32 = jnp.float32
BF16 = jnp.bfloat16
LANES = 128
SUB = 8
WROWS = 16
VM = pl.BlockSpec(memory_space=pltpu.VMEM)
HIGHEST = lax.Precision.HIGHEST


def params(mib):
    return pltpu.CompilerParams(vmem_limit_bytes=mib << 20)


def in_vmem(array):
    return pltpu.with_memory_space_constraint(array, pltpu.VMEM)


def in_hbm(array):
    return pltpu.with_memory_space_constraint(array, pltpu.HBM)


def split(values):
    high = values.astype(BF16)
    return high, (values - high.astype(F32)).astype(BF16)


def iota(shape, dim):
    return lax.broadcasted_iota(jnp.int32, shape, dim)


def coefficients(trace_map, lift_map, block):
    faces = trace_map.shape[0]
    width = block * block
    row = iota((block, width), 0)
    lane = iota((block, width), 1)
    first = lane // block == row
    second = lane % block == row
    spread_t = jnp.dot(trace_map, first.astype(F32), precision=HIGHEST)
    spread_l = jnp.dot(lift_map, second.astype(F32), precision=HIGHEST)
    rows = [jnp.where(second, spread_t[f : f + 1], 0.0) for f in range(faces)]
    rows += [jnp.where(first, spread_l[g : g + 1], 0.0) for g in range(faces)]
    rows += [spread_t[f : f + 1] * spread_l for f in range(faces)]
    rows.append(jnp.zeros((WROWS - faces * faces, width), F32))
    return jnp.concatenate(rows, axis=0)


def prepare(
    counts_hbm,
    inv_hbm,
    rhs_hbm,
    order_hbm,
    index_hbm,
    weights_hbm,
    trace_hbm,
    lift_hbm,
    r_out,
    w_out,
    il_out,
    q_out,
    inv,
    rhs,
    index,
    weights,
    live_out,
    p_out,
    counts,
    order,
    trace_map,
    lift_map,
    ti,
    stacked,
    sem,
):
    pairs = [
        (order_hbm, order),
        (trace_hbm, trace_map),
        (lift_hbm, lift_map),
        (inv_hbm, inv),
        (rhs_hbm, rhs),
        (index_hbm, index),
        (weights_hbm, weights),
        (counts_hbm, counts),
    ]
    copies = [pltpu.make_async_copy(a, b, sem.at[i]) for i, (a, b) in enumerate(pairs)]
    for copy in copies:
        copy.start()
    block, _, cells = inv.shape
    faces = trace_map.shape[0]
    tracers = rhs.shape[1]
    rows = faces * tracers
    half = rows + WROWS
    copies[0].wait()
    for j in range(cells // LANES):
        hit = iota((LANES, cells), 0) + j * LANES == order[...]
        q_out[j * LANES : (j + 1) * LANES, :] = jnp.where(hit, 1.0, 0.0).astype(BF16)
    copies[1].wait()
    copies[2].wait()
    high, low = split(coefficients(trace_map[...], lift_map[...], block))
    copies[3].wait()
    flat = inv[...].reshape(block * block, cells)
    made = jnp.dot(high, flat, preferred_element_type=F32) + jnp.dot(
        low, flat, preferred_element_type=F32
    )
    ti[...] = made[: faces * block]
    il_out[...] = made[faces * block : 2 * faces * block]
    high, low = split(made[2 * faces * block :])
    stacked[rows:half, :] = high
    stacked[half + rows :, :] = low
    copies[4].wait()
    for j in range(cells // LANES):
        at = pl.ds(j * LANES, LANES)
        sums = [None] * faces
        for b in range(block):
            source = rhs[b, :, at].astype(F32)
            for f in range(faces):
                term = ti[f * block + b : f * block + b + 1, at] * source
                sums[f] = term if sums[f] is None else sums[f] + term
        for f in range(faces):
            high, low = split(sums[f])
            stacked[f * tracers : (f + 1) * tracers, at] = high
            stacked[half + f * tracers : half + (f + 1) * tracers, at] = low
    slots = jnp.dot(stacked[...], q_out[...], preferred_element_type=F32)
    copies[7].wait()
    for level in range(cells // LANES):
        lo, hi = level * LANES, (level + 1) * LANES
        live = (iota((1, LANES), 1) < counts[level]).astype(F32)
        live_out[:, lo:hi] = live
        r_out[:, lo:hi] = (slots[:rows, lo:hi] + slots[half : half + rows, lo:hi]) * live
        w_out[:, lo:hi] = (slots[rows:half, lo:hi] + slots[half + rows :, lo:hi]) * live
    copies[5].wait()
    copies[6].wait()


def gathered(source, lane):
    return jnp.take_along_axis(source, lane, axis=1, mode="promise_in_bounds")


def face_values(faces_at, level, sources, index, count):
    at = index[faces_at : faces_at + 1, level * LANES : (level + 1) * LANES]
    at = jnp.broadcast_to(at, (SUB, LANES))
    lane = at & (LANES - 1)
    group = lax.shift_right_logical(at, LANES.bit_length() - 1)
    values = [None] * count
    for code, read in sources:
        here = group == code
        for i in range(count):
            got = gathered(read(i), lane)
            values[i] = jnp.where(here, got, 0.0 if values[i] is None else values[i])
    return values


def rows_of(i):
    return slice(i * SUB, (i + 1) * SUB)


def inflow_only(face, level):
    return face == 1 or (face == 0 and level == 0)


def rim_part(ring_a, ring_b, index, weights, e_out, rim, *, cross):
    column = lax.axis_index(cross)
    last = lax.axis_size(cross) - 1
    even = column % 2 == 0
    faces, cells = index.shape
    rows = e_out.shape[0]
    count = rows // SUB
    has_lower = column > 0
    has_upper = column < last
    lower = jnp.where(even, ring_b[1], ring_a[1])
    upper = jnp.where(even, ring_a[0], ring_b[0])
    rim[0] = jnp.where(has_lower, lower, 0.0)
    rim[1] = jnp.where(has_upper, upper, 0.0)
    for level in range(cells // LANES):
        at = slice(level * LANES, (level + 1) * LANES)
        sums = [None] * count
        for face in range(faces):
            if inflow_only(face, level):
                continue
            sources = [(1 + s, lambda i, s=s: rim[s, rows_of(i), :]) for s in range(2)]
            values = face_values(face, level, sources, index, count)
            weight = jnp.broadcast_to(weights[face : face + 1, at], (SUB, LANES))
            for i in range(count):
                term = values[i] * weight
                sums[i] = term if sums[i] is None else sums[i] + term
        for i in range(count):
            e_out[rows_of(i), at] = sums[i]


def sweep(inflow, r, w, index, weights, e_out, traces_out, pool, face_dofs):
    faces, cells = index.shape
    levels = cells // LANES
    count = e_out.shape[0] // SUB
    per_dof = count // face_dofs
    for level in range(levels):
        at = slice(level * LANES, (level + 1) * LANES)
        sums = [e_out[rows_of(i), at] for i in range(count)]
        for face in range(faces):
            sources = []
            if inflow is not None:
                sources.append((0, lambda i: inflow[rows_of(i), :]))
            if not inflow_only(face, level):
                sources += [
                    (3 + s, lambda i, s=s: pool[s, rows_of(i), :]) for s in range(level)
                ]
            if not sources:
                continue
            values = face_values(face, level, sources, index, count)
            weight = jnp.broadcast_to(weights[face : face + 1, at], (SUB, LANES))
            for i in range(count):
                sums[i] = sums[i] + values[i] * weight
        for i in range(count):
            e_out[rows_of(i), at] = sums[i]
        for f in range(face_dofs):
            mix = [
                jnp.broadcast_to(w[face_dofs * f + g : face_dofs * f + g + 1, at], (SUB, LANES))
                for g in range(face_dofs)
            ]
            for q in range(per_dof):
                i = f * per_dof + q
                value = r[rows_of(i), at]
                for g in range(face_dofs):
                    value = value + mix[g] * sums[g * per_dof + q]
                if level < levels - 1:
                    pool[level, rows_of(i), :] = value
                else:
                    traces_out[rows_of(i), :] = value


def local_group(j, live, inv, rhs, q, p_out, wide):
    block = inv.shape[0]
    cells = rhs.shape[2]
    start = pl.multiple_of(j * LANES, LANES)
    at = pl.ds(start, LANES)
    rows = jnp.broadcast_to(live[...], (WROWS, cells)).astype(BF16)
    mask = lax.dot_general(
        rows, q[at, :], (((1,), (1,)), ((), ())), preferred_element_type=F32
    )[:1]
    for a in range(block):
        wide[a * block : (a + 1) * block, :] = inv[a, :, at].astype(F32) * mask
    step = 4

    def some(part, carry):
        sums = [None] * step
        for b in range(block):
            source = rhs[b, :, at].astype(F32)
            for i in range(step):
                row = (part * step + i) * block + b
                term = wide[pl.ds(row, 1), :] * source
                sums[i] = term if sums[i] is None else sums[i] + term
        for i in range(step):
            p_out[part * step + i, :, at] = sums[i]
        return carry

    lax.fori_loop(0, block // step, some, 0)


def turn(*refs, moment, flow, face_dofs, last):
    refs = list(refs)
    inflow = refs.pop(0) if moment > 0 else None
    live, r, w, index, weights, inv, rhs, q, _, _, e_out, p_out, traces_out, pool, wide = refs
    position = lax.axis_index(flow)
    others = lax.axis_size(flow) - 1
    groups = index.shape[1] // LANES

    def some_groups(first, end):
        lax.fori_loop(
            first, end, lambda j, c: (local_group(j, live, inv, rhs, q, p_out, wide), c)[1], 0
        )

    @pl.when(position == moment)
    def _():
        sweep(inflow, r, w, index, weights, e_out, traces_out, pool, face_dofs)
        if others == 0:
            some_groups(0, groups)

    if others > 0:

        @pl.when(position != moment)
        def _():
            part = jnp.where(position < moment, moment - 1, moment)
            some_groups(part * groups // others, (part + 1) * groups // others)


def finish(live, e, p, il, q, out, stacked, done, sem):
    block, tracers, cells = p.shape
    rows = e.shape[0]
    face_dofs = rows // tracers
    high, low = split(e[...] * live[...])
    stacked[:rows, :] = high
    stacked[rows:, :] = low
    width = 2 * LANES
    copies = []
    for jj in range(cells // width):
        back = lax.dot_general(
            stacked[...],
            q[jj * width : (jj + 1) * width, :],
            (((1,), (1,)), ((), ())),
            preferred_element_type=F32,
        )
        for k in range(2):
            at = pl.ds(jj * width + k * LANES, LANES)
            part = slice(k * LANES, (k + 1) * LANES)
            carried = [
                back[g * tracers : (g + 1) * tracers, part]
                + back[rows + g * tracers : rows + (g + 1) * tracers, part]
                for g in range(face_dofs)
            ]
            for a in range(block):
                value = p[a, :, at]
                for g in range(face_dofs):
                    value = value + il[g * block + a : g * block + a + 1, at] * carried[g]
                done[a, :, at] = value
        at = pl.ds(jj * width, width)
        copy = pltpu.make_async_copy(done.at[:, :, at], out.at[:, :, at], sem.at[jj])
        copy.start()
        copies.append(copy)
    for copy in copies:
        copy.wait()


def swaps(flows, columns, partner):
    pairs = []
    for f in range(flows):
        for c in range(columns):
            to_f, to_c = partner(f, c)
            if not (0 <= to_f < flows and 0 <= to_c < columns):
                to_f, to_c = f, c
            pairs.append((f * columns + c, to_f * columns + to_c))
    return pairs


def rim_partner(first, columns):
    def partner(f, c):
        other = c + 1 if c % 2 == first else c - 1
        return (f, other) if 0 <= other < columns else (f ^ 1, c)

    return partner


def hop_partner(moment):
    def partner(f, c):
        return (2 * moment + 1 - f, c) if f in (moment, moment + 1) else (f, c ^ 1)

    return partner


def shards(
    rhs,
    inverses,
    flux_weights,
    upwind_index,
    sweep_order,
    level_counts,
    boundary_traces,
    trace_map,
    lift_map,
):
    _, _, block, tracers, cells = rhs.shape
    face_dofs = trace_map.shape[0]
    rows = face_dofs * tracers
    flows = lax.axis_size("flow")
    columns = lax.axis_size("cross")
    edges = boundary_traces.reshape(2, rows, LANES)
    axes = ("flow", "cross")
    ring_a = lax.ppermute(edges, axes, swaps(flows, columns, rim_partner(0, columns)))
    ring_b = lax.ppermute(edges, axes, swaps(flows, columns, rim_partner(1, columns)))
    faces = upwind_index.shape[2]
    far = pl.BlockSpec(memory_space=pltpu.HBM)

    r, w, il, q, inv, rhs, index, weights, live, p = pl.pallas_call(
        prepare,
        out_shape=(
            pltpu.VMEM((rows, cells), F32),
            pltpu.VMEM((WROWS, cells), F32),
            pltpu.VMEM((face_dofs * block, cells), F32),
            pltpu.VMEM((cells, cells), BF16),
            pltpu.VMEM((block, block, cells), BF16),
            pltpu.VMEM((block, tracers, cells), BF16),
            pltpu.VMEM((faces, cells), jnp.int32),
            pltpu.VMEM((faces, cells), F32),
            pltpu.VMEM((1, cells), F32),
            pltpu.VMEM((block, tracers, cells), F32),
        ),
        in_specs=[far] * 8,
        out_specs=(VM,) * 10,
        scratch_shapes=[
            pltpu.SMEM((cells // LANES,), jnp.int32),
            pltpu.VMEM((1, cells), jnp.int32),
            pltpu.VMEM((face_dofs, block), F32),
            pltpu.VMEM((face_dofs, block), F32),
            pltpu.VMEM((face_dofs * block, cells), F32),
            pltpu.VMEM((2 * (rows + WROWS), cells), BF16),
            pltpu.SemaphoreType.DMA((8,)),
        ],
        compiler_params=params(12),
        name="prepare",
    )(
        in_hbm(level_counts[0, 0]),
        in_hbm(inverses[0, 0]),
        in_hbm(rhs[0, 0]),
        in_hbm(sweep_order[0]),
        in_hbm(upwind_index[0, 0]),
        in_hbm(flux_weights[0, 0]),
        in_hbm(trace_map),
        in_hbm(lift_map.T),
    )

    e = pl.pallas_call(
        functools.partial(rim_part, cross="cross"),
        out_shape=pltpu.VMEM((rows, cells), F32),
        in_specs=[VM] * 4,
        out_specs=VM,
        scratch_shapes=[pltpu.VMEM((2, rows, LANES), F32)],
        compiler_params=params(4),
        name="rim",
    )(in_vmem(ring_a), in_vmem(ring_b), index, weights)

    received = None
    for moment in range(flows):
        last = moment == flows - 1
        given = [] if moment == 0 else [in_vmem(received)]
        n = len(given)
        given += [live, r, w, index, weights, inv, rhs, q, e, p]
        shapes = [
            pltpu.VMEM((rows, cells), F32),
            pltpu.VMEM((block, tracers, cells), F32),
        ]
        sent = pltpu.VMEM((rows, LANES), F32)
        made = pl.pallas_call(
            functools.partial(turn, moment=moment, flow="flow", face_dofs=face_dofs, last=last),
            out_shape=shapes if last else shapes + [sent],
            in_specs=[VM] * (n + 10),
            out_specs=[VM] * (2 if last else 3),
            input_output_aliases={len(given) - 2: 0, len(given) - 1: 1},
            scratch_shapes=([sent] if last else [])
            + [
                pltpu.VMEM((cells // LANES, rows, LANES), F32),
                pltpu.VMEM((block * block, LANES), F32),
            ],
            compiler_params=params(4),
            name=f"turn{moment}",
        )(*given)
        e, p = made[:2]
        if not last:
            received = lax.ppermute(
                made[2], axes, swaps(flows, columns, hop_partner(moment))
            )

    out = pl.pallas_call(
        finish,
        out_shape=jax.ShapeDtypeStruct((block, tracers, cells), F32),
        in_specs=[VM] * 5,
        out_specs=pl.BlockSpec(memory_space=pltpu.HBM),
        scratch_shapes=[
            pltpu.VMEM((2 * rows, cells), BF16),
            pltpu.VMEM((block, tracers, cells), F32),
            pltpu.SemaphoreType.DMA((cells // (2 * LANES),)),
        ],
        compiler_params=params(12),
        name="finish",
    )(live, e, p, il, q)
    return out[None, None]


def solution(mesh):
    placed = (
        P("flow", "cross", None, None, None),
        P("flow", "cross", None, None, None),
        P("flow", "cross", None, None),
        P("flow", "cross", None, None),
        P("flow", "cross", None),
        P("flow", "cross", None),
        P("flow", "cross", None, None, None),
        P(),
        P(),
    )
    return jax.shard_map(
        shards,
        mesh=mesh,
        in_specs=placed,
        out_specs=P("flow", "cross", None, None, None),
        check_vma=False,
    )
```

```python
import functools

import jax
import jax.numpy as jnp
from jax import lax
from jax.experimental import pallas as pl
from jax.experimental.pallas import tpu as pltpu
from jax.sharding import PartitionSpec as P

F32 = jnp.float32
BF16 = jnp.bfloat16
LANES = 128
SUB = 8
WROWS = 16
VM = pl.BlockSpec(memory_space=pltpu.VMEM)
HIGHEST = lax.Precision.HIGHEST


def params(mib):
    return pltpu.CompilerParams(vmem_limit_bytes=mib << 20)


def in_vmem(array):
    return pltpu.with_memory_space_constraint(array, pltpu.VMEM)


def in_hbm(array):
    return pltpu.with_memory_space_constraint(array, pltpu.HBM)


def split(values):
    high = values.astype(BF16)
    return high, (values - high.astype(F32)).astype(BF16)


def iota(shape, dim):
    return lax.broadcasted_iota(jnp.int32, shape, dim)


def coefficients(trace_map, lift_map, block):
    faces = trace_map.shape[0]
    width = block * block
    row = iota((block, width), 0)
    lane = iota((block, width), 1)
    first = lane // block == row
    second = lane % block == row
    spread_t = jnp.dot(trace_map, first.astype(F32), precision=HIGHEST)
    spread_l = jnp.dot(lift_map, second.astype(F32), precision=HIGHEST)
    rows = [jnp.where(second, spread_t[f : f + 1], 0.0) for f in range(faces)]
    rows += [jnp.where(first, spread_l[g : g + 1], 0.0) for g in range(faces)]
    rows += [spread_t[f : f + 1] * spread_l for f in range(faces)]
    rows.append(jnp.zeros((WROWS - faces * faces, width), F32))
    return jnp.concatenate(rows, axis=0)


def load(
    counts_hbm,
    inv_hbm,
    rhs_hbm,
    order_hbm,
    index_hbm,
    weights_hbm,
    trace_hbm,
    lift_hbm,
    ti,
    il,
    mix,
    q,
    inv,
    rhs,
    index,
    weights,
    live,
    p_out,
    carried_out,
    order,
    counts,
    trace_map,
    lift_map,
    sem,
):
    pairs = [
        (trace_hbm, trace_map),
        (lift_hbm, lift_map),
        (order_hbm, order),
        (inv_hbm, inv),
        (rhs_hbm, rhs),
        (index_hbm, index),
        (weights_hbm, weights),
        (counts_hbm, counts),
    ]
    copies = [pltpu.make_async_copy(a, b, sem.at[i]) for i, (a, b) in enumerate(pairs)]
    for copy in copies:
        copy.start()
    block, _, cells = inv.shape
    faces = trace_map.shape[0]
    for copy in copies[:3]:
        copy.wait()
    high, low = split(coefficients(trace_map[...], lift_map[...], block))
    for j in range(cells // LANES):
        hit = iota((LANES, cells), 0) + j * LANES == order[...]
        q[j * LANES : (j + 1) * LANES, :] = jnp.where(hit, 1.0, 0.0).astype(BF16)
    copies[7].wait()
    for level in range(cells // LANES):
        here = iota((1, LANES), 1) < counts[level]
        live[:, level * LANES : (level + 1) * LANES] = here.astype(F32)
    copies[3].wait()
    flat = inv[...].reshape(block * block, cells)
    made = jnp.dot(high, flat, preferred_element_type=F32) + jnp.dot(
        low, flat, preferred_element_type=F32
    )
    ti[...] = made[: faces * block]
    il[...] = made[faces * block : 2 * faces * block]
    high, low = split(made[2 * faces * block :])
    mix[:WROWS, :] = high
    mix[WROWS:, :] = low
    for copy in copies[4:7]:
        copy.wait()


def local_first(*refs, axes):
    flow, cross = axes

    @pl.when(lax.axis_index(flow) == 0)
    def _():
        local_work(*refs, cross=cross, first=True)


def local_rest(*refs, axes):
    flow, cross = axes
    order, qt = refs[9], refs[18]
    cells = qt.shape[0]
    for level in range(cells // LANES):
        at = slice(level * LANES, (level + 1) * LANES)
        spread = jnp.broadcast_to(order[:, at].astype(F32), (LANES, LANES)).T
        for j in range(cells // LANES):
            hit = spread == (iota((LANES, LANES), 1) + j * LANES).astype(F32)
            qt[at, j * LANES : (j + 1) * LANES] = jnp.where(hit, 1.0, 0.0).astype(BF16)

    @pl.when(lax.axis_index(flow) > 0)
    def _():
        local_work(*refs[:9], *refs[14:18], *refs[19:], cross=cross, first=False)


def local_work(
    ring_a,
    ring_b,
    ti,
    mix,
    rhs,
    q,
    live,
    index,
    weights,
    r_out,
    w_out,
    e_out,
    s_out,
    stacked,
    rim,
    *,
    cross,
    first,
):
    block, tracers, cells = rhs.shape
    rows = r_out.shape[0]
    faces = rows // tracers
    half = rows + WROWS
    stacked[rows:half, :] = mix[:WROWS, :]
    stacked[half + rows :, :] = mix[WROWS:, :]
    rim_sources(ring_a, ring_b, rim, cross)
    groups = cells // LANES
    slots = None
    for j in range(groups):
        at = pl.ds(j * LANES, LANES)
        sums = [None] * faces
        for b in range(block):
            source = rhs[b, :, at].astype(F32)
            for f in range(faces):
                term = ti[f * block + b : f * block + b + 1, at] * source
                sums[f] = term if sums[f] is None else sums[f] + term
        for f in range(faces):
            high, low = split(sums[f])
            stacked[f * tracers : (f + 1) * tracers, at] = high
            stacked[half + f * tracers : half + (f + 1) * tracers, at] = low
        rim_level(j, rim, index, weights, e_out)
        if (j + 1) % (groups // 2) == 0:
            part = pl.ds((j + 1 - groups // 2) * LANES, groups // 2 * LANES)
            term = jnp.dot(stacked[:, part], q[part, :], preferred_element_type=F32)
            slots = term if slots is None else slots + term
    slots = slots[:half] + slots[half:]
    r_out[...] = slots[:rows] * live[...]
    w_out[...] = slots[rows:] * live[...]
    if not first:
        for level in range(groups):
            inflow_weights(level, index, weights, s_out)


def gathered(source, lane):
    return jnp.take_along_axis(source, lane, axis=1, mode="promise_in_bounds")


def face_values(faces_at, level, sources, index, count):
    at = index[faces_at : faces_at + 1, level * LANES : (level + 1) * LANES]
    at = jnp.broadcast_to(at, (SUB, LANES))
    lane = at & (LANES - 1)
    group = lax.shift_right_logical(at, LANES.bit_length() - 1)
    values = [None] * count
    for code, read in sources:
        here = group == code
        for i in range(count):
            got = gathered(read(i), lane)
            values[i] = jnp.where(here, got, 0.0 if values[i] is None else values[i])
    return values


def rows_of(i):
    return slice(i * SUB, (i + 1) * SUB)


def inflow_only(face, level):
    return face == 1 or (face == 0 and level == 0)


def rim_sources(ring_a, ring_b, rim, cross):
    column = lax.axis_index(cross)
    last = lax.axis_size(cross) - 1
    even = column % 2 == 0
    lower = jnp.where(even, ring_b[1], ring_a[1])
    upper = jnp.where(even, ring_a[0], ring_b[0])
    rim[0] = jnp.where(column > 0, lower, 0.0)
    rim[1] = jnp.where(column < last, upper, 0.0)


def rim_level(level, rim, index, weights, e_out):
    count = e_out.shape[0] // SUB
    at = slice(level * LANES, (level + 1) * LANES)
    sums = [None] * count
    for face in range(index.shape[0]):
        if inflow_only(face, level):
            continue
        sources = [(1 + s, lambda i, s=s: rim[s, rows_of(i), :]) for s in range(2)]
        values = face_values(face, level, sources, index, count)
        weight = jnp.broadcast_to(weights[face : face + 1, at], (SUB, LANES))
        for i in range(count):
            term = values[i] * weight
            sums[i] = term if sums[i] is None else sums[i] + term
    for i in range(count):
        e_out[rows_of(i), at] = sums[i]


def inflow_weights(level, index, weights, s_out):
    at = slice(level * LANES, (level + 1) * LANES)
    source = iota((LANES, LANES), 0)
    total = None
    for face in range(index.shape[0]):
        hit = index[face : face + 1, at] == source
        term = jnp.where(hit, weights[face : face + 1, at], 0.0)
        total = term if total is None else total + term
    high, low = split(total)
    s_out[:, at] = high
    s_out[:, slice(s_out.shape[1] // 2 + at.start, s_out.shape[1] // 2 + at.stop)] = low


def sweep(
    inflow, live, r, w, index, weights, s, e, qt, back, traces_out, pool, ends, stacked, face_dofs
):
    faces, cells = index.shape
    levels = cells // LANES
    rows = e.shape[0]
    count = rows // SUB
    per_dof = count // face_dofs
    pair = 2 * LANES
    if inflow is not None:
        high, low = split(inflow[...])
        ends[:rows, :] = high
        ends[rows:, :] = low
    for level in range(levels):
        at = slice(level * LANES, (level + 1) * LANES)
        if inflow is not None and level % 2 == 0:
            both = slice(level * LANES, level * LANES + pair)
            main = jnp.dot(ends[...], s[:, both], preferred_element_type=F32)
            rest = jnp.dot(
                ends[:rows, :],
                s[:, slice(cells + both.start, cells + both.stop)],
                preferred_element_type=F32,
            )
            given = e[:, both] + (main[:rows] + (main[rows:] + rest))
        if inflow is None:
            sums = [e[rows_of(i), at] for i in range(count)]
        else:
            half = slice(level % 2 * LANES, (level % 2 + 1) * LANES)
            sums = [given[rows_of(i), half] for i in range(count)]
        for face in range(faces):
            if inflow_only(face, level) or level == 0:
                continue
            sources = [(3 + v, lambda i, v=v: pool[v, rows_of(i), :]) for v in range(level)]
            values = face_values(face, level, sources, index, count)
            weight = jnp.broadcast_to(weights[face : face + 1, at], (SUB, LANES))
            for i in range(count):
                sums[i] = sums[i] + values[i] * weight
        spot = at
        for i in range(0, count, 2):
            masked = jnp.concatenate([sums[i], sums[i + 1]], axis=0) * live[:, at]
            high, low = split(masked)
            stacked[i * SUB : (i + 2) * SUB, spot] = high
            stacked[rows + i * SUB : rows + (i + 2) * SUB, spot] = low
        for f in range(face_dofs):
            mix = [
                jnp.broadcast_to(w[face_dofs * f + g : face_dofs * f + g + 1, at], (SUB, LANES))
                for g in range(face_dofs)
            ]
            for k in range(per_dof):
                i = f * per_dof + k
                value = r[rows_of(i), at]
                for g in range(face_dofs):
                    value = value + mix[g] * sums[g * per_dof + k]
                if level < levels - 1:
                    pool[level, rows_of(i), :] = value
                else:
                    traces_out[rows_of(i), :] = value
        if back is not None and level % 2 == 1:
            both = slice((level - 1) * LANES, (level + 1) * LANES)
            moved = jnp.dot(stacked[:, both], qt[both, :], preferred_element_type=F32)
            moved = moved[:rows] + moved[rows:]
            back[...] = moved if level == 1 else back[...] + moved


def local_group(j, live, inv, rhs, q, p_out, wide):
    block = inv.shape[0]
    cells = rhs.shape[2]
    start = pl.multiple_of(j * LANES, LANES)
    at = pl.ds(start, LANES)
    rows = jnp.broadcast_to(live[...], (WROWS, cells)).astype(BF16)
    mask = lax.dot_general(
        rows, q[at, :], (((1,), (1,)), ((), ())), preferred_element_type=F32
    )[:1]
    for a in range(block):
        wide[a * block : (a + 1) * block, :] = inv[a, :, at].astype(F32) * mask
    step = 4

    def some(part, carry):
        sums = [None] * step
        for b in range(block):
            source = rhs[b, :, at].astype(F32)
            for i in range(step):
                row = (part * step + i) * block + b
                term = wide[pl.ds(row, 1), :] * source
                sums[i] = term if sums[i] is None else sums[i] + term
        for i in range(step):
            p_out[part * step + i, :, at] = sums[i]
        return carry

    lax.fori_loop(0, block // step, some, 0)


def local_plan(flows, groups):
    plan = []
    for f in range(flows):
        steps = [("turn", m) for m in range(f) if (f, m) != (1, 0)]
        steps += [("window", m) for m in range(max(f, min(1, flows - 2)), flows - 1)]
        steps = steps or [("final", flows - 1)]
        ends = [-(-k * groups // len(steps)) for k in range(len(steps) + 1)]
        plan.append({step: (ends[k], ends[k + 1]) for k, step in enumerate(steps)})
    return plan


def planned_groups(step, flow, live, inv, rhs, q, p_out, wide):
    flows = lax.axis_size(flow)
    plan = local_plan(flows, rhs.shape[2] // LANES)
    if not any(step in own for own in plan):
        return
    position = lax.axis_index(flow)
    first = end = 0
    for f in range(flows):
        low, high = plan[f].get(step, (0, 0))
        first = jnp.where(position == f, low, first)
        end = jnp.where(position == f, high, end)
    lax.fori_loop(
        first, end, lambda j, c: (local_group(j, live, inv, rhs, q, p_out, wide), c)[1], 0
    )


def turn(*refs, moment, flow, face_dofs, fused):
    refs = list(refs)
    inflow = refs.pop(0) if moment > 0 else None
    live, r, w, index, weights, e = refs[:6]
    refs = refs[6:]
    s = qt = ends = back = None
    if moment > 0:
        s, qt = refs[:2]
        refs = refs[2:]
    if fused:
        back, traces_out, stacked, pool, ends = refs
    else:
        inv, rhs, q, _, _, p_out, stacked, traces_out, pool, wide = refs[:10]
        ends = refs[10] if moment > 0 else None

    @pl.when(lax.axis_index(flow) == moment)
    def _():
        sweep(
            inflow,
            live,
            r,
            w,
            index,
            weights,
            s,
            e,
            qt,
            back,
            traces_out,
            pool,
            ends,
            stacked,
            face_dofs,
        )

    if not fused:
        planned_groups(("turn", moment), flow, live, inv, rhs, q, p_out, wide)


def window(live, inv, rhs, q, _, p_out, wide, *, moment, flow):
    planned_groups(("window", moment), flow, live, inv, rhs, q, p_out, wide)


def move_back(carried, qt, back):
    moved = jnp.dot(carried[...], qt[...], preferred_element_type=F32)
    rows = back.shape[0]
    back[...] = moved[:rows] + moved[rows:]


def early(live, inv, rhs, q, carried, qt, il, _, p, out, wide, back, done, sem, *, moment, flow):
    planned_groups(("window", moment), flow, live, inv, rhs, q, p, wide)

    @pl.when(lax.axis_index(flow) <= moment)
    def _():
        move_back(carried, qt, back)
        write_solution(back, p, il, out, done, sem)


def final(live, inv, rhs, q, back, qt, il, _, out_in, p, out, wide, moved, done, sem, *, flow, fused):
    last = lax.axis_size(flow) - 1
    planned_groups(("final", last), flow, live, inv, rhs, q, p, wide)

    @pl.when(lax.axis_index(flow) == last)
    def _():
        if not fused:
            move_back(back, qt, moved)
        write_solution(back if fused else moved, p, il, out, done, sem)


def write_solution(back, p, il, out, done, sem):
    block, tracers, cells = p.shape
    face_dofs = back.shape[0] // tracers
    copies = []
    for a in range(block):
        for j in range(cells // LANES):
            at = pl.ds(j * LANES, LANES)
            value = p[a, :, at]
            for g in range(face_dofs):
                scale = il[g * block + a : g * block + a + 1, at]
                value = value + scale * back[g * tracers : (g + 1) * tracers, at]
            done[a, :, at] = value
        copy = pltpu.make_async_copy(done.at[a], out.at[a], sem.at[a])
        copy.start()
        copies.append(copy)
    for copy in copies:
        copy.wait()


def swaps(flows, columns, partner):
    pairs = []
    for f in range(flows):
        for c in range(columns):
            to_f, to_c = partner(f, c)
            if not (0 <= to_f < flows and 0 <= to_c < columns):
                to_f, to_c = f, c
            pairs.append((f * columns + c, to_f * columns + to_c))
    return pairs


def rim_partner(first, columns):
    def partner(f, c):
        other = c + 1 if c % 2 == first else c - 1
        if columns % 2 == 0:
            other %= columns
        return f, other

    return partner


def hop_partner(moment):
    def partner(f, c):
        return (2 * moment + 1 - f, c) if f in (moment, moment + 1) else (f, c ^ 1)

    return partner


def shards(
    rhs,
    inverses,
    flux_weights,
    upwind_index,
    sweep_order,
    level_counts,
    boundary_traces,
    trace_map,
    lift_map,
):
    _, _, block, tracers, cells = rhs.shape
    face_dofs = trace_map.shape[0]
    rows = face_dofs * tracers
    flows = lax.axis_size("flow")
    columns = lax.axis_size("cross")
    edges = boundary_traces.reshape(2, rows, LANES)
    axes = ("flow", "cross")
    ring_a = lax.ppermute(edges, axes, swaps(flows, columns, rim_partner(0, columns)))
    ring_b = lax.ppermute(edges, axes, swaps(flows, columns, rim_partner(1, columns)))
    faces = upwind_index.shape[2]
    far = pl.BlockSpec(memory_space=pltpu.HBM)

    ti, il, mix, q, inv, rhs, index, weights, live, p, carried, order = pl.pallas_call(
        load,
        out_shape=(
            pltpu.VMEM((face_dofs * block, cells), F32),
            pltpu.VMEM((face_dofs * block, cells), F32),
            pltpu.VMEM((2 * WROWS, cells), BF16),
            pltpu.VMEM((cells, cells), BF16),
            pltpu.VMEM((block, block, cells), BF16),
            pltpu.VMEM((block, tracers, cells), BF16),
            pltpu.VMEM((faces, cells), jnp.int32),
            pltpu.VMEM((faces, cells), F32),
            pltpu.VMEM((1, cells), F32),
            pltpu.VMEM((block, tracers, cells), F32),
            pltpu.VMEM((2 * rows, cells), BF16),
            pltpu.VMEM((1, cells), jnp.int32),
        ),
        in_specs=[far] * 8,
        out_specs=(VM,) * 12,
        scratch_shapes=[
            pltpu.SMEM((cells // LANES,), jnp.int32),
            pltpu.VMEM((face_dofs, block), F32),
            pltpu.VMEM((face_dofs, block), F32),
            pltpu.SemaphoreType.DMA((8,)),
        ],
        compiler_params=params(12),
        name="load",
    )(
        in_hbm(level_counts[0, 0]),
        in_hbm(inverses[0, 0]),
        in_hbm(rhs[0, 0]),
        in_hbm(sweep_order[0]),
        in_hbm(upwind_index[0, 0]),
        in_hbm(flux_weights[0, 0]),
        in_hbm(trace_map),
        in_hbm(lift_map.T),
    )

    made_shapes = [
        pltpu.VMEM((rows, cells), F32),
        pltpu.VMEM((WROWS, cells), F32),
        pltpu.VMEM((rows, cells), F32),
        pltpu.VMEM((LANES, 2 * cells), BF16),
    ]
    local_scratch = [
        pltpu.VMEM((2 * (rows + WROWS), cells), BF16),
        pltpu.VMEM((2, rows, LANES), F32),
    ]
    local_given = [in_vmem(ring_a), in_vmem(ring_b), ti, mix, rhs, q, live, index, weights]
    r, w, e, s = pl.pallas_call(
        functools.partial(local_first, axes=axes),
        out_shape=made_shapes,
        in_specs=[VM] * 9,
        out_specs=[VM] * 4,
        scratch_shapes=local_scratch,
        compiler_params=params(12),
        name="local_first",
    )(*local_given)

    back_shape = pltpu.VMEM((rows, cells), F32)
    p_shape = pltpu.VMEM((block, tracers, cells), F32)
    halves = pltpu.VMEM((2 * rows, cells), BF16)
    sent = pltpu.VMEM((rows, LANES), F32)
    pool = pltpu.VMEM((cells // LANES, rows, LANES), F32)
    wide = pltpu.VMEM((block * block, LANES), F32)
    ends = pltpu.VMEM((2 * rows, LANES), BF16)
    out_shape = pltpu.HBM((block, tracers, cells), F32)
    out_scratch = [p_shape, pltpu.SemaphoreType.DMA((block,))]
    qt = received = out = back = None
    for moment in range(flows):
        last = moment == flows - 1
        fused = last and moment > 0
        given = [] if moment == 0 else [in_vmem(received)]
        given += [live, r, w, index, weights, e] + ([] if moment == 0 else [s, qt])
        more = [] if moment == 0 else [ends]
        run = functools.partial(
            turn, moment=moment, flow="flow", face_dofs=face_dofs, fused=fused
        )
        if fused:
            back = pl.pallas_call(
                run,
                out_shape=back_shape,
                in_specs=[VM] * len(given),
                out_specs=VM,
                scratch_shapes=[sent, halves, pool, ends],
                compiler_params=params(4),
                name=f"turn{moment}",
            )(*given)
            break
        given += [inv, rhs, q, p, carried]
        p, carried, traces = pl.pallas_call(
            run,
            out_shape=[p_shape, halves, sent],
            in_specs=[VM] * len(given),
            out_specs=[VM] * 3,
            input_output_aliases={len(given) - 2: 0, len(given) - 1: 1},
            scratch_shapes=[pool, wide] + more,
            compiler_params=params(4),
            name=f"turn{moment}",
        )(*given)
        if not last:
            received = lax.ppermute(traces, axes, swaps(flows, columns, hop_partner(moment)))
        if moment == 0:
            r, w, e, s, qt = pl.pallas_call(
                functools.partial(local_rest, axes=axes),
                out_shape=made_shapes + [pltpu.VMEM((cells, cells), BF16)],
                in_specs=[VM] * 14,
                out_specs=[VM] * 5,
                input_output_aliases={10: 0, 11: 1, 12: 2, 13: 3},
                scratch_shapes=local_scratch,
                compiler_params=params(12),
                name="local_rest",
            )(*local_given, order, r, w, e, s)
        if moment == flows - 2:
            p, out = pl.pallas_call(
                functools.partial(early, moment=moment, flow="flow"),
                out_shape=[p_shape, out_shape],
                in_specs=[VM] * 8,
                out_specs=[VM, far],
                input_output_aliases={7: 0},
                scratch_shapes=[wide, back_shape] + out_scratch,
                compiler_params=params(8),
                name="early",
            )(live, inv, rhs, q, carried, qt, il, p)
        elif 0 < moment < flows - 2:
            p = pl.pallas_call(
                functools.partial(window, moment=moment, flow="flow"),
                out_shape=p_shape,
                in_specs=[VM] * 5,
                out_specs=VM,
                input_output_aliases={4: 0},
                scratch_shapes=[wide],
                compiler_params=params(4),
                name=f"window{moment}",
            )(live, inv, rhs, q, p)

    if out is None:
        out = jnp.zeros((block, tracers, cells), F32)
    p, out = pl.pallas_call(
        functools.partial(final, flow="flow", fused=fused),
        out_shape=[p_shape, out_shape],
        in_specs=[VM] * 8 + [far],
        out_specs=[VM, far],
        input_output_aliases={7: 0, 8: 1},
        scratch_shapes=[wide, back_shape] + out_scratch,
        compiler_params=params(8),
        name="final",
    )(live, inv, rhs, q, back if fused else carried, qt, il, p, out)
    return out[None, None]


def solution(mesh):
    placed = (
        P("flow", "cross", None, None, None),
        P("flow", "cross", None, None, None),
        P("flow", "cross", None, None),
        P("flow", "cross", None, None),
        P("flow", "cross", None),
        P("flow", "cross", None),
        P("flow", "cross", None, None, None),
        P(),
        P(),
    )
    return jax.shard_map(
        shards,
        mesh=mesh,
        in_specs=placed,
        out_specs=P("flow", "cross", None, None, None),
        check_vma=False,
    )
```

```python
import functools

import jax
import jax.numpy as jnp
from jax import lax
from jax.experimental import pallas as pl
from jax.experimental.pallas import tpu as pltpu
from jax.sharding import PartitionSpec as P

F32 = jnp.float32
BF16 = jnp.bfloat16
LANES = 128
SUB = 8
WROWS = 16
LAG = 3
VM = pl.BlockSpec(memory_space=pltpu.VMEM)
HIGHEST = lax.Precision.HIGHEST


def params(mib):
    return pltpu.CompilerParams(vmem_limit_bytes=mib << 20)


def in_vmem(array):
    return pltpu.with_memory_space_constraint(array, pltpu.VMEM)


def in_hbm(array):
    return pltpu.with_memory_space_constraint(array, pltpu.HBM)


def split(values):
    high = values.astype(BF16)
    return high, (values - high.astype(F32)).astype(BF16)


def iota(shape, dim):
    return lax.broadcasted_iota(jnp.int32, shape, dim)


def coefficients(trace_map, lift_map, block):
    faces = trace_map.shape[0]
    width = block * block
    row = iota((block, width), 0)
    lane = iota((block, width), 1)
    first = lane // block == row
    second = lane % block == row
    spread_t = jnp.dot(trace_map, first.astype(F32), precision=HIGHEST)
    spread_l = jnp.dot(lift_map, second.astype(F32), precision=HIGHEST)
    rows = [jnp.where(second, spread_t[f : f + 1], 0.0) for f in range(faces)]
    rows += [jnp.where(first, spread_l[g : g + 1], 0.0) for g in range(faces)]
    rows += [spread_t[f : f + 1] * spread_l for f in range(faces)]
    rows.append(jnp.zeros((WROWS - faces * faces, width), F32))
    return jnp.concatenate(rows, axis=0)


def load(
    counts_hbm,
    inv_hbm,
    rhs_hbm,
    order_hbm,
    index_hbm,
    weights_hbm,
    trace_hbm,
    lift_hbm,
    ti,
    il,
    mix,
    q,
    inv,
    rhs,
    index,
    weights,
    live,
    p_out,
    carried_out,
    order,
    counts,
    trace_map,
    lift_map,
    sem,
):
    pairs = [
        (trace_hbm, trace_map),
        (lift_hbm, lift_map),
        (order_hbm, order),
        (inv_hbm, inv),
        (rhs_hbm, rhs),
        (index_hbm, index),
        (weights_hbm, weights),
        (counts_hbm, counts),
    ]
    copies = [pltpu.make_async_copy(a, b, sem.at[i]) for i, (a, b) in enumerate(pairs)]
    for copy in copies:
        copy.start()
    block, _, cells = inv.shape
    faces = trace_map.shape[0]
    for copy in copies[:3]:
        copy.wait()
    high, low = split(coefficients(trace_map[...], lift_map[...], block))
    for j in range(cells // LANES):
        hit = iota((LANES, cells), 0) + j * LANES == order[...]
        q[j * LANES : (j + 1) * LANES, :] = jnp.where(hit, 1.0, 0.0).astype(BF16)
    copies[7].wait()
    for level in range(cells // LANES):
        here = iota((1, LANES), 1) < counts[level]
        live[:, level * LANES : (level + 1) * LANES] = here.astype(F32)
    copies[3].wait()
    flat = inv[...].reshape(block * block, cells)
    made = jnp.dot(high, flat, preferred_element_type=F32) + jnp.dot(
        low, flat, preferred_element_type=F32
    )
    ti[...] = made[: faces * block]
    il[...] = made[faces * block : 2 * faces * block]
    high, low = split(made[2 * faces * block :])
    mix[:WROWS, :] = high
    mix[WROWS:, :] = low
    for copy in copies[4:7]:
        copy.wait()


def products(ti, mix, rhs, q, live, r_out, w_out, stacked):
    block, tracers, cells = rhs.shape
    rows = r_out.shape[0]
    faces = rows // tracers
    half = rows + WROWS
    stacked[rows:half, :] = mix[:WROWS, :]
    stacked[half + rows :, :] = mix[WROWS:, :]
    groups = cells // LANES
    slots = None
    for j in range(groups):
        at = pl.ds(j * LANES, LANES)
        sums = [None] * faces
        for b in range(block):
            source = rhs[b, :, at].astype(F32)
            for f in range(faces):
                term = ti[f * block + b : f * block + b + 1, at] * source
                sums[f] = term if sums[f] is None else sums[f] + term
        for f in range(faces):
            high, low = split(sums[f])
            stacked[f * tracers : (f + 1) * tracers, at] = high
            stacked[half + f * tracers : half + (f + 1) * tracers, at] = low
        if (j + 1) % (groups // 2) == 0:
            part = pl.ds((j + 1 - groups // 2) * LANES, groups // 2 * LANES)
            term = jnp.dot(stacked[:, part], q[part, :], preferred_element_type=F32)
            slots = term if slots is None else slots + term
    slots = slots[:half] + slots[half:]
    r_out[...] = slots[:rows] * live[...]
    w_out[...] = slots[rows:] * live[...]


def rim_first(ring_a, ring_b, index, weights, e_out, rim, *, axes):
    flow, cross = axes

    @pl.when(lax.axis_index(flow) == 0)
    def _():
        rim_sources(ring_a, ring_b, rim, cross)
        for level in range(index.shape[1] // LANES):
            rim_level(level, rim, index, weights, e_out)


def rim_rest(ring_a, ring_b, index, weights, order, _, e_out, s_out, own, qt, rim, *, axes):
    flow, cross = axes
    cells = qt.shape[0]
    for level in range(cells // LANES):
        at = slice(level * LANES, (level + 1) * LANES)
        spread = jnp.broadcast_to(order[:, at].astype(F32), (LANES, LANES)).T
        for j in range(cells // LANES):
            hit = spread == (iota((LANES, LANES), 1) + j * LANES).astype(F32)
            qt[at, j * LANES : (j + 1) * LANES] = jnp.where(hit, 1.0, 0.0).astype(BF16)

    @pl.when(lax.axis_index(flow) > 0)
    def _():
        rim_sources(ring_a, ring_b, rim, cross)
        for level in range(cells // LANES):
            rim_level(level, rim, index, weights, e_out)
            inflow_weights(level, index, weights, s_out)
            own_weights(level, index, weights, own)


def gathered(source, lane):
    return jnp.take_along_axis(source, lane, axis=1, mode="promise_in_bounds")


def face_values(faces_at, level, sources, index, count):
    at = index[faces_at : faces_at + 1, level * LANES : (level + 1) * LANES]
    at = jnp.broadcast_to(at, (SUB, LANES))
    lane = at & (LANES - 1)
    group = lax.shift_right_logical(at, LANES.bit_length() - 1)
    values = [None] * count
    for code, read in sources:
        here = group == code
        for i in range(count):
            got = gathered(read(i), lane)
            values[i] = jnp.where(here, got, 0.0 if values[i] is None else values[i])
    return values


def rows_of(i):
    return slice(i * SUB, (i + 1) * SUB)


def inflow_only(face, level):
    return face == 1 or (face == 0 and level == 0)


def rim_sources(ring_a, ring_b, rim, cross):
    column = lax.axis_index(cross)
    last = lax.axis_size(cross) - 1
    even = column % 2 == 0
    lower = jnp.where(even, ring_b[1], ring_a[1])
    upper = jnp.where(even, ring_a[0], ring_b[0])
    rim[0] = jnp.where(column > 0, lower, 0.0)
    rim[1] = jnp.where(column < last, upper, 0.0)


def rim_level(level, rim, index, weights, e_out):
    count = e_out.shape[0] // SUB
    at = slice(level * LANES, (level + 1) * LANES)
    sums = [None] * count
    for face in range(index.shape[0]):
        if inflow_only(face, level):
            continue
        sources = [(1 + s, lambda i, s=s: rim[s, rows_of(i), :]) for s in range(2)]
        values = face_values(face, level, sources, index, count)
        weight = jnp.broadcast_to(weights[face : face + 1, at], (SUB, LANES))
        for i in range(count):
            term = values[i] * weight
            sums[i] = term if sums[i] is None else sums[i] + term
    for i in range(count):
        e_out[rows_of(i), at] = sums[i]


def inflow_weights(level, index, weights, s_out):
    at = slice(level * LANES, (level + 1) * LANES)
    source = iota((LANES, LANES), 0)
    total = None
    for face in range(index.shape[0]):
        hit = index[face : face + 1, at] == source
        term = jnp.where(hit, weights[face : face + 1, at], 0.0)
        total = term if total is None else total + term
    high, low = split(total)
    s_out[:, at] = high
    s_out[:, slice(s_out.shape[1] // 2 + at.start, s_out.shape[1] // 2 + at.stop)] = low


def older_rows(level):
    return sum(max(v - LAG + 1, 0) for v in range(level)) * LANES


def own_weights(level, index, weights, own):
    depth = (level - LAG + 1) * LANES
    if depth <= 0:
        return
    at = slice(level * LANES, (level + 1) * LANES)
    source = iota((depth, LANES), 0) + 3 * LANES
    total = None
    for face in range(index.shape[0]):
        if inflow_only(face, level):
            continue
        hit = index[face : face + 1, at] == source
        term = jnp.where(hit, weights[face : face + 1, at], 0.0)
        total = term if total is None else total + term
    high, low = split(total)
    start = older_rows(level)
    own[start : start + depth, :LANES] = high
    own[start : start + depth, LANES:] = low


def sweep(
    inflow, live, r, w, index, weights, s, own, e, traces_out, pool, ends, narrow, stacked, face_dofs
):
    faces, cells = index.shape
    levels = cells // LANES
    rows = e.shape[0]
    count = rows // SUB
    per_dof = count // face_dofs
    pair = 2 * LANES
    if inflow is not None:
        high, low = split(inflow[...])
        ends[:rows, :] = high
        ends[rows:, :] = low
    for level in range(levels):
        at = slice(level * LANES, (level + 1) * LANES)
        if inflow is not None and level % 2 == 0:
            both = slice(level * LANES, level * LANES + pair)
            main = jnp.dot(ends[...], s[:, both], preferred_element_type=F32)
            rest = jnp.dot(
                ends[:rows, :],
                s[:, slice(cells + both.start, cells + both.stop)],
                preferred_element_type=F32,
            )
            given = e[:, both] + (main[:rows] + (main[rows:] + rest))
        if inflow is None:
            sums = [e[rows_of(i), at] for i in range(count)]
        else:
            half = slice(level % 2 * LANES, (level % 2 + 1) * LANES)
            sums = [given[rows_of(i), half] for i in range(count)]
        oldest = 0
        if own is not None and level >= LAG:
            oldest = level - LAG + 1
            start = older_rows(level)
            got = jnp.dot(
                narrow[:, : oldest * LANES],
                own[start : start + oldest * LANES, :],
                preferred_element_type=F32,
            )
            got = got[:rows, :LANES] + (got[rows:, :LANES] + got[:rows, LANES:])
            sums = [sums[i] + got[rows_of(i), :] for i in range(count)]
        for face in range(faces):
            if inflow_only(face, level) or level == 0:
                continue
            sources = [
                (3 + v, lambda i, v=v: pool[v, rows_of(i), :])
                for v in range(oldest, level)
            ]
            values = face_values(face, level, sources, index, count)
            weight = jnp.broadcast_to(weights[face : face + 1, at], (SUB, LANES))
            for i in range(count):
                sums[i] = sums[i] + values[i] * weight
        spot = at
        for i in range(0, count, 2):
            masked = jnp.concatenate([sums[i], sums[i + 1]], axis=0) * live[:, at]
            high, low = split(masked)
            stacked[i * SUB : (i + 2) * SUB, spot] = high
            stacked[rows + i * SUB : rows + (i + 2) * SUB, spot] = low
        for f in range(face_dofs):
            mix = [
                jnp.broadcast_to(w[face_dofs * f + g : face_dofs * f + g + 1, at], (SUB, LANES))
                for g in range(face_dofs)
            ]
            for k in range(per_dof):
                i = f * per_dof + k
                value = r[rows_of(i), at]
                for g in range(face_dofs):
                    value = value + mix[g] * sums[g * per_dof + k]
                if level < levels - 1:
                    pool[level, rows_of(i), :] = value
                else:
                    traces_out[rows_of(i), :] = value
        if own is not None and level < levels - LAG:
            high, low = split(pool[level])
            narrow[:rows, at] = high
            narrow[rows:, at] = low


def local_group(j, live, inv, rhs, q, p_out, wide):
    block = inv.shape[0]
    cells = rhs.shape[2]
    start = pl.multiple_of(j * LANES, LANES)
    at = pl.ds(start, LANES)
    rows = jnp.broadcast_to(live[...], (WROWS, cells)).astype(BF16)
    mask = lax.dot_general(
        rows, q[at, :], (((1,), (1,)), ((), ())), preferred_element_type=F32
    )[:1]
    for a in range(block):
        wide[a * block : (a + 1) * block, :] = inv[a, :, at].astype(F32) * mask
    step = block // 2

    def some(part, carry):
        sums = [None] * step
        for b in range(block):
            source = rhs[b, :, at].astype(F32)
            for i in range(step):
                row = (part * step + i) * block + b
                term = wide[pl.ds(row, 1), :] * source
                sums[i] = term if sums[i] is None else sums[i] + term
        for i in range(step):
            p_out[part * step + i, :, at] = sums[i]
        return carry

    lax.fori_loop(0, block // step, some, 0)


def local_plan(flows, groups):
    plan = []
    for f in range(flows):
        turns = [("turn", m) for m in range(f if f > 2 else f - 1)]
        late = [("window", m) for m in range(max(f, min(1, flows - 2)), flows - 1)]
        steps = turns + late or [("final", flows - 1)]
        shares = [1] * len(turns) + [2] * len(late) or [1]
        ends = [-(-sum(shares[:k]) * groups // sum(shares)) for k in range(len(steps) + 1)]
        plan.append({step: (ends[k], ends[k + 1]) for k, step in enumerate(steps)})
    return plan


def planned_groups(step, flow, live, inv, rhs, q, p_out, wide):
    flows = lax.axis_size(flow)
    plan = local_plan(flows, rhs.shape[2] // LANES)
    if not any(step in own for own in plan):
        return
    position = lax.axis_index(flow)
    first = end = 0
    for f in range(flows):
        low, high = plan[f].get(step, (0, 0))
        first = jnp.where(position == f, low, first)
        end = jnp.where(position == f, high, end)
    lax.fori_loop(
        first, end, lambda j, c: (local_group(j, live, inv, rhs, q, p_out, wide), c)[1], 0
    )


def turn(*refs, moment, flow, face_dofs):
    refs = list(refs)
    inflow = refs.pop(0) if moment > 0 else None
    live, r, w, index, weights, e = refs[:6]
    s, own = (refs.pop(6), refs.pop(6)) if moment > 0 else (None, None)
    inv, rhs, q, _, _, p_out, stacked, traces_out, pool, wide = refs[6:16]
    ends, narrow = refs[16:] if moment > 0 else (None, None)

    @pl.when(lax.axis_index(flow) == moment)
    def _():
        sweep(
            inflow,
            live,
            r,
            w,
            index,
            weights,
            s,
            own,
            e,
            traces_out,
            pool,
            ends,
            narrow,
            stacked,
            face_dofs,
        )

    planned_groups(("turn", moment), flow, live, inv, rhs, q, p_out, wide)


def window(live, inv, rhs, q, _, p_out, wide, *, moment, flow):
    planned_groups(("window", moment), flow, live, inv, rhs, q, p_out, wide)


def early(live, inv, rhs, q, carried, qt, il, _, p, out, wide, done, sem, *, moment, flow):
    planned_groups(("window", moment), flow, live, inv, rhs, q, p, wide)

    @pl.when(lax.axis_index(flow) <= moment)
    def _():
        write_solution(carried, qt, p, il, out, done, sem)


def final(live, inv, rhs, q, carried, qt, il, _, out_in, p, out, wide, done, sem, *, flow):
    last = lax.axis_size(flow) - 1
    planned_groups(("final", last), flow, live, inv, rhs, q, p, wide)

    @pl.when(lax.axis_index(flow) == last)
    def _():
        write_solution(carried, qt, p, il, out, done, sem)


def write_solution(carried, qt, p, il, out, done, sem):
    block, tracers, cells = p.shape
    rows = carried.shape[0] // 2
    face_dofs = rows // tracers
    width = 2 * LANES
    parts = cells // width

    def copy_of(part):
        at = pl.ds(pl.multiple_of(part * width, width), width)
        return pltpu.make_async_copy(done.at[:, :, at], out.at[:, :, at], sem.at[part])

    def moved_to(part):
        cols = pl.ds(pl.multiple_of(part * width, width), width)
        back = jnp.dot(carried[...], qt[:, cols], preferred_element_type=F32)
        return back[:rows] + back[rows:]

    def write(part, moved):
        for k in range(2):
            at = pl.ds(pl.multiple_of(part * width + k * LANES, LANES), LANES)
            half = slice(k * LANES, (k + 1) * LANES)
            for a in range(block):
                value = p[a, :, at]
                for g in range(face_dofs):
                    scale = il[g * block + a : g * block + a + 1, at]
                    value = value + scale * moved[g * tracers : (g + 1) * tracers, half]
                done[a, :, at] = value
        copy_of(part).start()

    def one(part, moved):
        following = moved_to(part + 1)
        write(part, moved)
        return following

    write(parts - 1, lax.fori_loop(0, parts - 1, one, moved_to(0)))
    for part in range(parts):
        copy_of(part).wait()


def swaps(flows, columns, partner):
    pairs = []
    for f in range(flows):
        for c in range(columns):
            to_f, to_c = partner(f, c)
            if not (0 <= to_f < flows and 0 <= to_c < columns):
                to_f, to_c = f, c
            pairs.append((f * columns + c, to_f * columns + to_c))
    return pairs


def rim_partner(first, columns):
    def partner(f, c):
        other = c + 1 if c % 2 == first else c - 1
        return (f, other) if 0 <= other < columns else (f ^ 1, c)

    return partner


def hop_partner(moment):
    def partner(f, c):
        return (2 * moment + 1 - f, c) if f in (moment, moment + 1) else (f, c ^ 1)

    return partner


def shards(
    rhs,
    inverses,
    flux_weights,
    upwind_index,
    sweep_order,
    level_counts,
    boundary_traces,
    trace_map,
    lift_map,
):
    _, _, block, tracers, cells = rhs.shape
    face_dofs = trace_map.shape[0]
    rows = face_dofs * tracers
    flows = lax.axis_size("flow")
    columns = lax.axis_size("cross")
    edges = boundary_traces.reshape(2, rows, LANES)
    axes = ("flow", "cross")
    ring_a = lax.ppermute(edges, axes, swaps(flows, columns, rim_partner(0, columns)))
    ring_b = lax.ppermute(edges, axes, swaps(flows, columns, rim_partner(1, columns)))
    faces = upwind_index.shape[2]
    far = pl.BlockSpec(memory_space=pltpu.HBM)

    ti, il, mix, q, inv, rhs, index, weights, live, p, carried, order = pl.pallas_call(
        load,
        out_shape=(
            pltpu.VMEM((face_dofs * block, cells), F32),
            pltpu.VMEM((face_dofs * block, cells), F32),
            pltpu.VMEM((2 * WROWS, cells), BF16),
            pltpu.VMEM((cells, cells), BF16),
            pltpu.VMEM((block, block, cells), BF16),
            pltpu.VMEM((block, tracers, cells), BF16),
            pltpu.VMEM((faces, cells), jnp.int32),
            pltpu.VMEM((faces, cells), F32),
            pltpu.VMEM((1, cells), F32),
            pltpu.VMEM((block, tracers, cells), F32),
            pltpu.VMEM((2 * rows, cells), BF16),
            pltpu.VMEM((1, cells), jnp.int32),
        ),
        in_specs=[far] * 8,
        out_specs=(VM,) * 12,
        scratch_shapes=[
            pltpu.SMEM((cells // LANES,), jnp.int32),
            pltpu.VMEM((face_dofs, block), F32),
            pltpu.VMEM((face_dofs, block), F32),
            pltpu.SemaphoreType.DMA((8,)),
        ],
        compiler_params=params(12),
        name="load",
    )(
        in_hbm(level_counts[0, 0]),
        in_hbm(inverses[0, 0]),
        in_hbm(rhs[0, 0]),
        in_hbm(sweep_order[0]),
        in_hbm(upwind_index[0, 0]),
        in_hbm(flux_weights[0, 0]),
        in_hbm(trace_map),
        in_hbm(lift_map.T),
    )

    e_shape = pltpu.VMEM((rows, cells), F32)
    rim_shape = pltpu.VMEM((2, rows, LANES), F32)
    p_shape = pltpu.VMEM((block, tracers, cells), F32)
    halves = pltpu.VMEM((2 * rows, cells), BF16)
    sent = pltpu.VMEM((rows, LANES), F32)
    pool = pltpu.VMEM((cells // LANES, rows, LANES), F32)
    wide = pltpu.VMEM((block * block, LANES), F32)
    ends = pltpu.VMEM((2 * rows, LANES), BF16)
    out_shape = pltpu.HBM((block, tracers, cells), F32)
    out_scratch = [wide, p_shape, pltpu.SemaphoreType.DMA((cells // (2 * LANES),))]

    r, w = pl.pallas_call(
        products,
        out_shape=[pltpu.VMEM((rows, cells), F32), pltpu.VMEM((WROWS, cells), F32)],
        in_specs=[VM] * 5,
        out_specs=[VM] * 2,
        scratch_shapes=[pltpu.VMEM((2 * (rows + WROWS), cells), BF16)],
        compiler_params=params(8),
        name="products",
    )(ti, mix, rhs, q, live)
    rim_given = [in_vmem(ring_a), in_vmem(ring_b), index, weights]
    e = pl.pallas_call(
        functools.partial(rim_first, axes=axes),
        out_shape=e_shape,
        in_specs=[VM] * 4,
        out_specs=VM,
        scratch_shapes=[rim_shape],
        compiler_params=params(4),
        name="rim_first",
    )(*rim_given)

    s = own = qt = received = out = None
    for moment in range(flows):
        last = moment == flows - 1
        given = [] if moment == 0 else [in_vmem(received)]
        given += [live, r, w, index, weights, e] + ([] if moment == 0 else [s, own])
        given += [inv, rhs, q, p, carried]
        made = pl.pallas_call(
            functools.partial(turn, moment=moment, flow="flow", face_dofs=face_dofs),
            out_shape=[p_shape, halves] + ([] if last else [sent]),
            in_specs=[VM] * len(given),
            out_specs=[VM] * (2 if last else 3),
            input_output_aliases={len(given) - 2: 0, len(given) - 1: 1},
            scratch_shapes=([sent] if last else [])
            + [pool, wide]
            + ([] if moment == 0 else [ends, halves]),
            compiler_params=params(4),
            name=f"turn{moment}",
        )(*given)
        p, carried = made[:2]
        if not last:
            received = lax.ppermute(made[2], axes, swaps(flows, columns, hop_partner(moment)))
        if moment == 0:
            e, s, own, qt = pl.pallas_call(
                functools.partial(rim_rest, axes=axes),
                out_shape=[
                    e_shape,
                    pltpu.VMEM((LANES, 2 * cells), BF16),
                    pltpu.VMEM((max(older_rows(cells // LANES), LANES), 2 * LANES), BF16),
                    pltpu.VMEM((cells, cells), BF16),
                ],
                in_specs=[VM] * 6,
                out_specs=[VM] * 4,
                input_output_aliases={5: 0},
                scratch_shapes=[rim_shape],
                compiler_params=params(8),
                name="rim_rest",
            )(*rim_given, order, e)
        if moment == flows - 2:
            p, out = pl.pallas_call(
                functools.partial(early, moment=moment, flow="flow"),
                out_shape=[p_shape, out_shape],
                in_specs=[VM] * 8,
                out_specs=[VM, far],
                input_output_aliases={7: 0},
                scratch_shapes=out_scratch,
                compiler_params=params(8),
                name="early",
            )(live, inv, rhs, q, carried, qt, il, p)
        elif 0 < moment < flows - 2:
            p = pl.pallas_call(
                functools.partial(window, moment=moment, flow="flow"),
                out_shape=p_shape,
                in_specs=[VM] * 5,
                out_specs=VM,
                input_output_aliases={4: 0},
                scratch_shapes=[wide],
                compiler_params=params(4),
                name=f"window{moment}",
            )(live, inv, rhs, q, p)

    if out is None:
        out = jnp.zeros((block, tracers, cells), F32)
    p, out = pl.pallas_call(
        functools.partial(final, flow="flow"),
        out_shape=[p_shape, out_shape],
        in_specs=[VM] * 8 + [far],
        out_specs=[VM, far],
        input_output_aliases={7: 0, 8: 1},
        scratch_shapes=out_scratch,
        compiler_params=params(8),
        name="final",
    )(live, inv, rhs, q, carried, qt, il, p, out)
    return out[None, None]


def solution(mesh):
    placed = (
        P("flow", "cross", None, None, None),
        P("flow", "cross", None, None, None),
        P("flow", "cross", None, None),
        P("flow", "cross", None, None),
        P("flow", "cross", None),
        P("flow", "cross", None),
        P("flow", "cross", None, None, None),
        P(),
        P(),
    )
    return jax.shard_map(
        shards,
        mesh=mesh,
        in_specs=placed,
        out_specs=P("flow", "cross", None, None, None),
        check_vma=False,
    )
```

```python
import functools

import jax
import jax.numpy as jnp
from jax import lax
from jax.experimental import pallas as pl
from jax.experimental.pallas import tpu as pltpu
from jax.sharding import PartitionSpec as P

F32 = jnp.float32
BF16 = jnp.bfloat16
LANES = 128
SUB = 8
WROWS = 16
LAG = 3
VM = pl.BlockSpec(memory_space=pltpu.VMEM)
HIGHEST = lax.Precision.HIGHEST


def params(mib):
    return pltpu.CompilerParams(vmem_limit_bytes=mib << 20)


def in_vmem(array):
    return pltpu.with_memory_space_constraint(array, pltpu.VMEM)


def in_hbm(array):
    return pltpu.with_memory_space_constraint(array, pltpu.HBM)


def split(values):
    high = values.astype(BF16)
    return high, (values - high.astype(F32)).astype(BF16)


def iota(shape, dim):
    return lax.broadcasted_iota(jnp.int32, shape, dim)


def coefficients(trace_map, lift_map, block):
    faces = trace_map.shape[0]
    width = block * block
    row = iota((block, width), 0)
    lane = iota((block, width), 1)
    first = lane // block == row
    second = lane % block == row
    spread_t = jnp.dot(trace_map, first.astype(F32), precision=HIGHEST)
    spread_l = jnp.dot(lift_map, second.astype(F32), precision=HIGHEST)
    rows = [jnp.where(second, spread_t[f : f + 1], 0.0) for f in range(faces)]
    rows += [jnp.where(first, spread_l[g : g + 1], 0.0) for g in range(faces)]
    rows += [spread_t[f : f + 1] * spread_l for f in range(faces)]
    rows.append(jnp.zeros((WROWS - faces * faces, width), F32))
    return jnp.concatenate(rows, axis=0)


def load(
    counts_hbm,
    inv_hbm,
    rhs_hbm,
    order_hbm,
    index_hbm,
    weights_hbm,
    trace_hbm,
    lift_hbm,
    ti,
    il,
    mix,
    q,
    inv,
    rhs,
    index,
    weights,
    live,
    p_out,
    carried_out,
    order,
    counts,
    trace_map,
    lift_map,
    sem,
):
    pairs = [
        (trace_hbm, trace_map),
        (lift_hbm, lift_map),
        (order_hbm, order),
        (inv_hbm, inv),
        (rhs_hbm, rhs),
        (index_hbm, index),
        (weights_hbm, weights),
        (counts_hbm, counts),
    ]
    copies = [pltpu.make_async_copy(a, b, sem.at[i]) for i, (a, b) in enumerate(pairs)]
    for copy in copies:
        copy.start()
    block, _, cells = inv.shape
    faces = trace_map.shape[0]
    for copy in copies[:3]:
        copy.wait()
    high, low = split(coefficients(trace_map[...], lift_map[...], block))
    groups = cells // LANES

    def mark(first, end):
        for j in range(first, end):
            hit = iota((LANES, cells), 0) + j * LANES == order[...]
            q[j * LANES : (j + 1) * LANES, :] = jnp.where(hit, 1.0, 0.0).astype(BF16)

    mark(0, groups)
    copies[7].wait()
    for level in range(cells // LANES):
        here = iota((1, LANES), 1) < counts[level]
        live[:, level * LANES : (level + 1) * LANES] = here.astype(F32)
    copies[3].wait()
    flat = inv[...].reshape(block * block, cells)
    made = jnp.dot(high, flat, preferred_element_type=F32) + jnp.dot(
        low, flat, preferred_element_type=F32
    )
    ti[...] = made[: faces * block]
    il[...] = made[faces * block : 2 * faces * block]
    high, low = split(made[2 * faces * block :])
    mix[:WROWS, :] = high
    mix[WROWS:, :] = low
    for copy in copies[4:7]:
        copy.wait()


def products(ti, mix, rhs, q, live, index, weights, r_out, w_out, own, stacked):
    block, tracers, cells = rhs.shape
    rows = r_out.shape[0]
    faces = rows // tracers
    half = rows + WROWS
    stacked[rows:half, :] = mix[:WROWS, :]
    stacked[half + rows :, :] = mix[WROWS:, :]
    groups = cells // LANES
    slots = None
    for j in range(groups):
        at = pl.ds(j * LANES, LANES)
        sums = [None] * faces
        for b in range(block):
            source = rhs[b, :, at].astype(F32)
            for f in range(faces):
                term = ti[f * block + b : f * block + b + 1, at] * source
                sums[f] = term if sums[f] is None else sums[f] + term
        for f in range(faces):
            high, low = split(sums[f])
            stacked[f * tracers : (f + 1) * tracers, at] = high
            stacked[half + f * tracers : half + (f + 1) * tracers, at] = low
        if (j + 1) % (groups // 4) == 0:
            part = pl.ds((j + 1 - groups // 4) * LANES, groups // 4 * LANES)
            term = jnp.dot(stacked[:, part], q[part, :], preferred_element_type=F32)
            slots = term if slots is None else slots + term
    for level in range(groups):
        own_weights(level, index, weights, own)
    slots = slots[:half] + slots[half:]
    r_out[...] = slots[:rows] * live[...]
    w_out[...] = slots[rows:] * live[...]


def rim_first(ring_a, ring_b, index, weights, e_out, rim, *, axes):
    flow, cross = axes

    @pl.when(lax.axis_index(flow) == 0)
    def _():
        rim_sources(ring_a, ring_b, rim, cross)
        for level in range(index.shape[1] // LANES):
            rim_level(level, rim, index, weights, e_out)


def storage_order(order, live, qt, mask):
    cells = qt.shape[0]
    for level in range(cells // LANES):
        at = slice(level * LANES, (level + 1) * LANES)
        spread = jnp.broadcast_to(order[:, at].astype(F32), (LANES, LANES)).T
        for j in range(cells // LANES):
            hit = spread == (iota((LANES, LANES), 1) + j * LANES).astype(F32)
            qt[at, j * LANES : (j + 1) * LANES] = jnp.where(hit, 1.0, 0.0).astype(BF16)
    rows = jnp.broadcast_to(live[...], (WROWS, cells)).astype(BF16)
    mask[...] = jnp.dot(rows, qt[...], preferred_element_type=F32)[:1]


def order_second(order, live, qt_in, mask_in, qt, mask, *, flow):
    @pl.when(lax.axis_index(flow) == 1)
    def _():
        storage_order(order, live, qt, mask)


def rim_rest(
    ring_a, ring_b, index, weights, order, live, _, e_out, s_out, qt, mask, rim, *, axes
):
    flow, cross = axes

    @pl.when(lax.axis_index(flow) != 1)
    def _():
        storage_order(order, live, qt, mask)

    @pl.when(lax.axis_index(flow) > 0)
    def _():
        rim_sources(ring_a, ring_b, rim, cross)
        for level in range(index.shape[1] // LANES):
            rim_level(level, rim, index, weights, e_out)
            inflow_weights(level, index, weights, s_out)


def gathered(source, lane):
    return jnp.take_along_axis(source, lane, axis=1, mode="promise_in_bounds")


def face_values(faces_at, level, sources, index, count):
    at = index[faces_at : faces_at + 1, level * LANES : (level + 1) * LANES]
    at = jnp.broadcast_to(at, (SUB, LANES))
    lane = at & (LANES - 1)
    group = lax.shift_right_logical(at, LANES.bit_length() - 1)
    values = [None] * count
    for code, read in sources:
        here = group == code
        for i in range(count):
            got = gathered(read(i), lane)
            values[i] = jnp.where(here, got, 0.0 if values[i] is None else values[i])
    return values


def rows_of(i):
    return slice(i * SUB, (i + 1) * SUB)


def inflow_only(face, level):
    return face == 1 or (face == 0 and level == 0)


def rim_sources(ring_a, ring_b, rim, cross):
    column = lax.axis_index(cross)
    last = lax.axis_size(cross) - 1
    even = column % 2 == 0
    lower = jnp.where(even, ring_b[1], ring_a[1])
    upper = jnp.where(even, ring_a[0], ring_b[0])
    rim[0] = jnp.where(column > 0, lower, 0.0)
    rim[1] = jnp.where(column < last, upper, 0.0)


def rim_level(level, rim, index, weights, e_out):
    count = e_out.shape[0] // SUB
    at = slice(level * LANES, (level + 1) * LANES)
    sums = [None] * count
    for face in range(index.shape[0]):
        if inflow_only(face, level):
            continue
        sources = [(1 + s, lambda i, s=s: rim[s, rows_of(i), :]) for s in range(2)]
        values = face_values(face, level, sources, index, count)
        weight = jnp.broadcast_to(weights[face : face + 1, at], (SUB, LANES))
        for i in range(count):
            term = values[i] * weight
            sums[i] = term if sums[i] is None else sums[i] + term
    for i in range(count):
        e_out[rows_of(i), at] = sums[i]


def inflow_weights(level, index, weights, s_out):
    at = slice(level * LANES, (level + 1) * LANES)
    source = iota((LANES, LANES), 0)
    total = None
    for face in range(index.shape[0]):
        hit = index[face : face + 1, at] == source
        term = jnp.where(hit, weights[face : face + 1, at], 0.0)
        total = term if total is None else total + term
    high, low = split(total)
    s_out[:, at] = high
    s_out[:, slice(s_out.shape[1] // 2 + at.start, s_out.shape[1] // 2 + at.stop)] = low


def older_rows(level):
    return sum(max(v - LAG + 1, 0) for v in range(level)) * LANES


def own_weights(level, index, weights, own):
    depth = (level - LAG + 1) * LANES
    if depth <= 0:
        return
    at = slice(level * LANES, (level + 1) * LANES)
    source = iota((depth, LANES), 0) + 3 * LANES
    total = None
    for face in range(index.shape[0]):
        if inflow_only(face, level):
            continue
        hit = index[face : face + 1, at] == source
        term = jnp.where(hit, weights[face : face + 1, at], 0.0)
        total = term if total is None else total + term
    high, low = split(total)
    start = older_rows(level)
    own[start : start + depth, :LANES] = high
    own[start : start + depth, LANES:] = low


def sweep(
    inflow, live, r, w, index, weights, s, own, e, traces_out, pool, ends, narrow, stacked, face_dofs
):
    faces, cells = index.shape
    levels = cells // LANES
    rows = e.shape[0]
    count = rows // SUB
    per_dof = count // face_dofs
    pair = 2 * LANES
    if inflow is not None:
        high, low = split(inflow[...])
        ends[:rows, :] = high
        ends[rows:, :] = low
    for level in range(levels):
        at = slice(level * LANES, (level + 1) * LANES)
        if inflow is not None and level % 2 == 0:
            both = slice(level * LANES, level * LANES + pair)
            main = jnp.dot(ends[...], s[:, both], preferred_element_type=F32)
            rest = jnp.dot(
                ends[:rows, :],
                s[:, slice(cells + both.start, cells + both.stop)],
                preferred_element_type=F32,
            )
            given = e[:, both] + (main[:rows] + (main[rows:] + rest))
        if inflow is None:
            sums = [e[rows_of(i), at] for i in range(count)]
        else:
            half = slice(level % 2 * LANES, (level % 2 + 1) * LANES)
            sums = [given[rows_of(i), half] for i in range(count)]
        oldest = 0
        if own is not None and level >= LAG:
            oldest = level - LAG + 1
            start = older_rows(level)
            got = jnp.dot(
                narrow[:, : oldest * LANES],
                own[start : start + oldest * LANES, :],
                preferred_element_type=F32,
            )
            got = got[:rows, :LANES] + (got[rows:, :LANES] + got[:rows, LANES:])
            sums = [sums[i] + got[rows_of(i), :] for i in range(count)]
        for face in range(faces):
            if inflow_only(face, level) or level == 0:
                continue
            sources = [
                (3 + v, lambda i, v=v: pool[v, rows_of(i), :])
                for v in range(oldest, level)
            ]
            values = face_values(face, level, sources, index, count)
            weight = jnp.broadcast_to(weights[face : face + 1, at], (SUB, LANES))
            for i in range(count):
                sums[i] = sums[i] + values[i] * weight
        spot = at
        for i in range(0, count, 2):
            masked = jnp.concatenate([sums[i], sums[i + 1]], axis=0) * live[:, at]
            high, low = split(masked)
            stacked[i * SUB : (i + 2) * SUB, spot] = high
            stacked[rows + i * SUB : rows + (i + 2) * SUB, spot] = low
        for f in range(face_dofs):
            mix = [
                jnp.broadcast_to(w[face_dofs * f + g : face_dofs * f + g + 1, at], (SUB, LANES))
                for g in range(face_dofs)
            ]
            for k in range(per_dof):
                i = f * per_dof + k
                value = r[rows_of(i), at]
                for g in range(face_dofs):
                    value = value + mix[g] * sums[g * per_dof + k]
                if level < levels - 1:
                    pool[level, rows_of(i), :] = value
                else:
                    traces_out[rows_of(i), :] = value
        if own is not None and level < levels - LAG:
            high, low = split(pool[level])
            narrow[:rows, at] = high
            narrow[rows:, at] = low


def local_group(j, mask, inv, rhs, p_out, wide):
    block = inv.shape[0]
    start = pl.multiple_of(j * LANES, LANES)
    at = pl.ds(start, LANES)
    for a in range(block):
        wide[a * block : (a + 1) * block, :] = inv[a, :, at].astype(F32) * mask[:, at]
    step = block // 2

    def some(part, carry):
        sums = [None] * step
        for b in range(block):
            source = rhs[b, :, at].astype(F32)
            for i in range(step):
                row = (part * step + i) * block + b
                term = wide[pl.ds(row, 1), :] * source
                sums[i] = term if sums[i] is None else sums[i] + term
        for i in range(step):
            p_out[part * step + i, :, at] = sums[i]
        return carry

    lax.fori_loop(0, block // step, some, 0)


def local_plan(flows, groups):
    plan = []
    for f in range(flows):
        turns = [("turn", m) for m in range(1, f if f > 2 else f - 1)]
        late = [("window", m) for m in range(max(f, min(1, flows - 2)), flows - 1)]
        steps = turns + late or [("final", flows - 1)]
        shares = [1] * len(turns) + [3] * len(late) or [1]
        ends = [-(-sum(shares[:k]) * groups // sum(shares)) for k in range(len(steps) + 1)]
        plan.append({step: (ends[k], ends[k + 1]) for k, step in enumerate(steps)})
    return plan


def planned_groups(step, flow, mask, inv, rhs, p_out, wide):
    flows = lax.axis_size(flow)
    plan = local_plan(flows, rhs.shape[2] // LANES)
    if not any(step in own for own in plan):
        return
    position = lax.axis_index(flow)
    first = end = 0
    for f in range(flows):
        low, high = plan[f].get(step, (0, 0))
        first = jnp.where(position == f, low, first)
        end = jnp.where(position == f, high, end)
    lax.fori_loop(
        first, end, lambda j, c: (local_group(j, mask, inv, rhs, p_out, wide), c)[1], 0
    )


def turn(*refs, moment, flow, face_dofs):
    refs = list(refs)
    inflow = refs.pop(0) if moment > 0 else None
    live, r, w, index, weights, e, own = refs[:7]
    s, mask = (refs.pop(7), refs.pop(7)) if moment > 0 else (None, None)
    inv, rhs, _, _, p_out, stacked, traces_out, pool, wide, narrow = refs[7:17]
    ends = refs[17] if moment > 0 else None

    @pl.when(lax.axis_index(flow) == moment)
    def _():
        sweep(
            inflow,
            live,
            r,
            w,
            index,
            weights,
            s,
            own,
            e,
            traces_out,
            pool,
            ends,
            narrow,
            stacked,
            face_dofs,
        )

    planned_groups(("turn", moment), flow, mask, inv, rhs, p_out, wide)


def window(mask, inv, rhs, _, p_out, wide, *, moment, flow):
    planned_groups(("window", moment), flow, mask, inv, rhs, p_out, wide)


def early(mask, inv, rhs, carried, qt, il, _, p, out, wide, done, sem, *, moment, flow):
    planned_groups(("window", moment), flow, mask, inv, rhs, p, wide)

    @pl.when(lax.axis_index(flow) <= moment)
    def _():
        write_solution(carried, qt, p, il, out, done, sem)


def final(mask, inv, rhs, carried, qt, il, _, out_in, p, out, wide, done, sem, *, flow):
    last = lax.axis_size(flow) - 1
    planned_groups(("final", last), flow, mask, inv, rhs, p, wide)

    @pl.when(lax.axis_index(flow) == last)
    def _():
        write_solution(carried, qt, p, il, out, done, sem)


def write_solution(carried, qt, p, il, out, done, sem):
    block, tracers, cells = p.shape
    rows = carried.shape[0] // 2
    face_dofs = rows // tracers
    width = 2 * LANES
    parts = cells // width

    def copy_of(part):
        at = pl.ds(pl.multiple_of(part * width, width), width)
        return pltpu.make_async_copy(done.at[:, :, at], out.at[:, :, at], sem.at[part])

    def moved_to(part):
        cols = pl.ds(pl.multiple_of(part * width, width), width)
        back = jnp.dot(carried[...], qt[:, cols], preferred_element_type=F32)
        return back[:rows] + back[rows:]

    def write(part, moved):
        for k in range(2):
            at = pl.ds(pl.multiple_of(part * width + k * LANES, LANES), LANES)
            half = slice(k * LANES, (k + 1) * LANES)
            for a in range(block):
                value = p[a, :, at]
                for g in range(face_dofs):
                    scale = il[g * block + a : g * block + a + 1, at]
                    value = value + scale * moved[g * tracers : (g + 1) * tracers, half]
                done[a, :, at] = value
        copy_of(part).start()

    def one(part, moved):
        following = moved_to(part + 1)
        write(part, moved)
        return following

    write(parts - 1, lax.fori_loop(0, parts - 1, one, moved_to(0)))
    for part in range(parts):
        copy_of(part).wait()


def swaps(flows, columns, partner):
    pairs = []
    for f in range(flows):
        for c in range(columns):
            to_f, to_c = partner(f, c)
            if not (0 <= to_f < flows and 0 <= to_c < columns):
                to_f, to_c = f, c
            pairs.append((f * columns + c, to_f * columns + to_c))
    return pairs


def rim_partner(first, columns):
    def partner(f, c):
        other = c + 1 if c % 2 == first else c - 1
        return (f, other) if 0 <= other < columns else (f ^ 1, c)

    return partner


def hop_partner(moment):
    def partner(f, c):
        return (2 * moment + 1 - f, c) if f in (moment, moment + 1) else (f, c ^ 1)

    return partner


def shards(
    rhs,
    inverses,
    flux_weights,
    upwind_index,
    sweep_order,
    level_counts,
    boundary_traces,
    trace_map,
    lift_map,
):
    _, _, block, tracers, cells = rhs.shape
    face_dofs = trace_map.shape[0]
    rows = face_dofs * tracers
    flows = lax.axis_size("flow")
    columns = lax.axis_size("cross")
    edges = boundary_traces.reshape(2, rows, LANES)
    axes = ("flow", "cross")
    ring_a = lax.ppermute(edges, axes, swaps(flows, columns, rim_partner(0, columns)))
    ring_b = lax.ppermute(edges, axes, swaps(flows, columns, rim_partner(1, columns)))
    faces = upwind_index.shape[2]
    far = pl.BlockSpec(memory_space=pltpu.HBM)

    ti, il, mix, q, inv, rhs, index, weights, live, p, carried, order = pl.pallas_call(
        load,
        out_shape=(
            pltpu.VMEM((face_dofs * block, cells), F32),
            pltpu.VMEM((face_dofs * block, cells), F32),
            pltpu.VMEM((2 * WROWS, cells), BF16),
            pltpu.VMEM((cells, cells), BF16),
            pltpu.VMEM((block, block, cells), BF16),
            pltpu.VMEM((block, tracers, cells), BF16),
            pltpu.VMEM((faces, cells), jnp.int32),
            pltpu.VMEM((faces, cells), F32),
            pltpu.VMEM((1, cells), F32),
            pltpu.VMEM((block, tracers, cells), F32),
            pltpu.VMEM((2 * rows, cells), BF16),
            pltpu.VMEM((1, cells), jnp.int32),
        ),
        in_specs=[far] * 8,
        out_specs=(VM,) * 12,
        scratch_shapes=[
            pltpu.SMEM((cells // LANES,), jnp.int32),
            pltpu.VMEM((face_dofs, block), F32),
            pltpu.VMEM((face_dofs, block), F32),
            pltpu.SemaphoreType.DMA((8,)),
        ],
        compiler_params=params(12),
        name="load",
    )(
        in_hbm(level_counts[0, 0]),
        in_hbm(inverses[0, 0]),
        in_hbm(rhs[0, 0]),
        in_hbm(sweep_order[0]),
        in_hbm(upwind_index[0, 0]),
        in_hbm(flux_weights[0, 0]),
        in_hbm(trace_map),
        in_hbm(lift_map.T),
    )

    e_shape = pltpu.VMEM((rows, cells), F32)
    rim_shape = pltpu.VMEM((2, rows, LANES), F32)
    p_shape = pltpu.VMEM((block, tracers, cells), F32)
    halves = pltpu.VMEM((2 * rows, cells), BF16)
    sent = pltpu.VMEM((rows, LANES), F32)
    pool = pltpu.VMEM((cells // LANES, rows, LANES), F32)
    wide = pltpu.VMEM((block * block, LANES), F32)
    ends = pltpu.VMEM((2 * rows, LANES), BF16)
    out_shape = pltpu.HBM((block, tracers, cells), F32)
    out_scratch = [wide, p_shape, pltpu.SemaphoreType.DMA((cells // (2 * LANES),))]

    r, w, own = pl.pallas_call(
        products,
        out_shape=[
            pltpu.VMEM((rows, cells), F32),
            pltpu.VMEM((WROWS, cells), F32),
            pltpu.VMEM((max(older_rows(cells // LANES), LANES), 2 * LANES), BF16),
        ],
        in_specs=[VM] * 7,
        out_specs=[VM] * 3,
        scratch_shapes=[pltpu.VMEM((2 * (rows + WROWS), cells), BF16)],
        compiler_params=params(8),
        name="products",
    )(ti, mix, rhs, q, live, index, weights)
    rim_given = [in_vmem(ring_a), in_vmem(ring_b), index, weights]
    e = pl.pallas_call(
        functools.partial(rim_first, axes=axes),
        out_shape=e_shape,
        in_specs=[VM] * 4,
        out_specs=VM,
        scratch_shapes=[rim_shape],
        compiler_params=params(4),
        name="rim_first",
    )(*rim_given)

    s = qt = mask = received = out = None
    for moment in range(flows):
        last = moment == flows - 1
        given = [] if moment == 0 else [in_vmem(received)]
        given += [live, r, w, index, weights, e, own] + ([] if moment == 0 else [s, mask])
        given += [inv, rhs, p, carried]
        made = pl.pallas_call(
            functools.partial(turn, moment=moment, flow="flow", face_dofs=face_dofs),
            out_shape=[p_shape, halves] + ([] if last else [sent]),
            in_specs=[VM] * len(given),
            out_specs=[VM] * (2 if last else 3),
            input_output_aliases={len(given) - 2: 0, len(given) - 1: 1},
            scratch_shapes=([sent] if last else [])
            + [pool, wide, halves]
            + ([] if moment == 0 else [ends]),
            compiler_params=params(4),
            name=f"turn{moment}",
        )(*given)
        p, carried = made[:2]
        if not last:
            received = lax.ppermute(made[2], axes, swaps(flows, columns, hop_partner(moment)))
        if moment == 0:
            e, s, qt, mask = pl.pallas_call(
                functools.partial(rim_rest, axes=axes),
                out_shape=[
                    e_shape,
                    pltpu.VMEM((LANES, 2 * cells), BF16),
                    pltpu.VMEM((cells, cells), BF16),
                    pltpu.VMEM((1, cells), F32),
                ],
                in_specs=[VM] * 7,
                out_specs=[VM] * 4,
                input_output_aliases={6: 0},
                scratch_shapes=[rim_shape],
                compiler_params=params(8),
                name="rim_rest",
            )(*rim_given, order, live, e)
        if moment == 1:
            qt, mask = pl.pallas_call(
                functools.partial(order_second, flow="flow"),
                out_shape=[
                    pltpu.VMEM((cells, cells), BF16),
                    pltpu.VMEM((1, cells), F32),
                ],
                in_specs=[VM] * 4,
                out_specs=[VM] * 2,
                input_output_aliases={2: 0, 3: 1},
                compiler_params=params(4),
                name="order_second",
            )(order, live, qt, mask)
        if moment == flows - 2:
            p, out = pl.pallas_call(
                functools.partial(early, moment=moment, flow="flow"),
                out_shape=[p_shape, out_shape],
                in_specs=[VM] * 7,
                out_specs=[VM, far],
                input_output_aliases={6: 0},
                scratch_shapes=out_scratch,
                compiler_params=params(8),
                name="early",
            )(mask, inv, rhs, carried, qt, il, p)
        elif 0 < moment < flows - 2:
            p = pl.pallas_call(
                functools.partial(window, moment=moment, flow="flow"),
                out_shape=p_shape,
                in_specs=[VM] * 4,
                out_specs=VM,
                input_output_aliases={3: 0},
                scratch_shapes=[wide],
                compiler_params=params(4),
                name=f"window{moment}",
            )(mask, inv, rhs, p)

    if out is None:
        out = jnp.zeros((block, tracers, cells), F32)
    p, out = pl.pallas_call(
        functools.partial(final, flow="flow"),
        out_shape=[p_shape, out_shape],
        in_specs=[VM] * 7 + [far],
        out_specs=[VM, far],
        input_output_aliases={6: 0, 7: 1},
        scratch_shapes=out_scratch,
        compiler_params=params(8),
        name="final",
    )(mask, inv, rhs, carried, qt, il, p, out)
    return out[None, None]


def solution(mesh):
    placed = (
        P("flow", "cross", None, None, None),
        P("flow", "cross", None, None, None),
        P("flow", "cross", None, None),
        P("flow", "cross", None, None),
        P("flow", "cross", None),
        P("flow", "cross", None),
        P("flow", "cross", None, None, None),
        P(),
        P(),
    )
    return jax.shard_map(
        shards,
        mesh=mesh,
        in_specs=placed,
        out_specs=P("flow", "cross", None, None, None),
        check_vma=False,
    )
```

```python
import functools

import jax
import jax.numpy as jnp
from jax import lax
from jax.experimental import pallas as pl
from jax.experimental.pallas import tpu as pltpu
from jax.sharding import PartitionSpec as P

F32 = jnp.float32
BF16 = jnp.bfloat16
LANES = 128
SUB = 8
WROWS = 16
LAG = 3
VM = pl.BlockSpec(memory_space=pltpu.VMEM)
HIGHEST = lax.Precision.HIGHEST


def params(mib):
    return pltpu.CompilerParams(vmem_limit_bytes=mib << 20)


def in_vmem(array):
    return pltpu.with_memory_space_constraint(array, pltpu.VMEM)


def in_hbm(array):
    return pltpu.with_memory_space_constraint(array, pltpu.HBM)


def split(values):
    high = values.astype(BF16)
    return high, (values - high.astype(F32)).astype(BF16)


def iota(shape, dim):
    return lax.broadcasted_iota(jnp.int32, shape, dim)


def coefficients(trace_map, lift_map, block):
    faces = trace_map.shape[0]
    width = block * block
    row = iota((block, width), 0)
    lane = iota((block, width), 1)
    first = lane // block == row
    second = lane % block == row
    spread_t = jnp.dot(trace_map, first.astype(F32), precision=HIGHEST)
    spread_l = jnp.dot(lift_map, second.astype(F32), precision=HIGHEST)
    rows = [jnp.where(second, spread_t[f : f + 1], 0.0) for f in range(faces)]
    rows += [jnp.where(first, spread_l[g : g + 1], 0.0) for g in range(faces)]
    rows += [spread_t[f : f + 1] * spread_l for f in range(faces)]
    rows.append(jnp.zeros((WROWS - faces * faces, width), F32))
    return jnp.concatenate(rows, axis=0)


def load(
    counts_hbm,
    inv_hbm,
    rhs_hbm,
    order_hbm,
    index_hbm,
    weights_hbm,
    trace_hbm,
    lift_hbm,
    ti,
    il,
    mix,
    q,
    inv,
    rhs,
    index,
    weights,
    live,
    p_out,
    carried_out,
    order,
    counts,
    trace_map,
    lift_map,
    sem,
):
    pairs = [
        (trace_hbm, trace_map),
        (lift_hbm, lift_map),
        (order_hbm, order),
        (inv_hbm, inv),
        (rhs_hbm, rhs),
        (index_hbm, index),
        (weights_hbm, weights),
        (counts_hbm, counts),
    ]
    copies = [pltpu.make_async_copy(a, b, sem.at[i]) for i, (a, b) in enumerate(pairs)]
    for copy in copies:
        copy.start()
    block, _, cells = inv.shape
    faces = trace_map.shape[0]
    for copy in copies[:3]:
        copy.wait()
    high, low = split(coefficients(trace_map[...], lift_map[...], block))
    groups = cells // LANES

    def mark(first, end):
        for j in range(first, end):
            hit = iota((LANES, cells), 0) + j * LANES == order[...]
            q[j * LANES : (j + 1) * LANES, :] = jnp.where(hit, 1.0, 0.0).astype(BF16)

    mark(0, groups)
    copies[7].wait()
    for level in range(cells // LANES):
        here = iota((1, LANES), 1) < counts[level]
        live[:, level * LANES : (level + 1) * LANES] = here.astype(F32)
    copies[3].wait()
    flat = inv[...].reshape(block * block, cells)
    made = jnp.dot(high, flat, preferred_element_type=F32) + jnp.dot(
        low, flat, preferred_element_type=F32
    )
    ti[...] = made[: faces * block]
    il[...] = made[faces * block : 2 * faces * block]
    high, low = split(made[2 * faces * block :])
    mix[:WROWS, :] = high
    mix[WROWS:, :] = low
    for copy in copies[4:7]:
        copy.wait()


def products(ti, mix, rhs, q, live, index, weights, r_out, w_out, own, stacked):
    block, tracers, cells = rhs.shape
    rows = r_out.shape[0]
    faces = rows // tracers
    half = rows + WROWS
    stacked[rows:half, :] = mix[:WROWS, :]
    stacked[half + rows :, :] = mix[WROWS:, :]
    groups = cells // LANES
    slots = None
    for j in range(groups):
        at = pl.ds(j * LANES, LANES)
        sums = [None] * faces
        for b in range(block):
            source = rhs[b, :, at].astype(F32)
            for f in range(faces):
                term = ti[f * block + b : f * block + b + 1, at] * source
                sums[f] = term if sums[f] is None else sums[f] + term
        for f in range(faces):
            high, low = split(sums[f])
            stacked[f * tracers : (f + 1) * tracers, at] = high
            stacked[half + f * tracers : half + (f + 1) * tracers, at] = low
        own_weights(j, index, weights, own)
        if (j + 1) % (groups // 4) == 0:
            part = pl.ds((j + 1 - groups // 4) * LANES, groups // 4 * LANES)
            term = jnp.dot(stacked[:, part], q[part, :], preferred_element_type=F32)
            slots = term if slots is None else slots + term
    slots = slots[:half] + slots[half:]
    r_out[...] = slots[:rows] * live[...]
    w_out[...] = slots[rows:] * live[...]


def rim_first(ring_a, ring_b, index, weights, e_out, rim, *, axes):
    flow, cross = axes

    @pl.when(lax.axis_index(flow) == 0)
    def _():
        rim_sources(ring_a, ring_b, rim, cross)
        for level in range(index.shape[1] // LANES):
            rim_level(level, rim, index, weights, e_out)


def storage_order(order, live, qt, mask):
    cells = qt.shape[0]
    for level in range(cells // LANES):
        at = slice(level * LANES, (level + 1) * LANES)
        spread = jnp.broadcast_to(order[:, at].astype(F32), (LANES, LANES)).T
        for j in range(cells // LANES):
            hit = spread == (iota((LANES, LANES), 1) + j * LANES).astype(F32)
            qt[at, j * LANES : (j + 1) * LANES] = jnp.where(hit, 1.0, 0.0).astype(BF16)
    rows = jnp.broadcast_to(live[...], (WROWS, cells)).astype(BF16)
    mask[...] = jnp.dot(rows, qt[...], preferred_element_type=F32)[:1]


def order_second(order, live, qt_in, mask_in, qt, mask, *, flow):
    @pl.when(lax.axis_index(flow) == 1)
    def _():
        storage_order(order, live, qt, mask)


def rim_rest(
    ring_a, ring_b, index, weights, order, live, _, e_out, s_out, qt, mask, rim, *, axes
):
    flow, cross = axes

    @pl.when(lax.axis_index(flow) != 1)
    def _():
        storage_order(order, live, qt, mask)

    @pl.when(lax.axis_index(flow) > 0)
    def _():
        rim_sources(ring_a, ring_b, rim, cross)
        for level in range(index.shape[1] // LANES):
            rim_level(level, rim, index, weights, e_out)
            inflow_weights(level, index, weights, s_out)


def gathered(source, lane):
    return jnp.take_along_axis(source, lane, axis=1, mode="promise_in_bounds")


def face_values(faces_at, level, sources, index, count):
    at = index[faces_at : faces_at + 1, level * LANES : (level + 1) * LANES]
    at = jnp.broadcast_to(at, (SUB, LANES))
    lane = at & (LANES - 1)
    group = lax.shift_right_logical(at, LANES.bit_length() - 1)
    values = [None] * count
    for code, read in sources:
        here = group == code
        for i in range(count):
            got = gathered(read(i), lane)
            values[i] = jnp.where(here, got, 0.0 if values[i] is None else values[i])
    return values


def rows_of(i):
    return slice(i * SUB, (i + 1) * SUB)


def inflow_only(face, level):
    return face == 1 or (face == 0 and level == 0)


def rim_sources(ring_a, ring_b, rim, cross):
    column = lax.axis_index(cross)
    last = lax.axis_size(cross) - 1
    even = column % 2 == 0
    lower = jnp.where(even, ring_b[1], ring_a[1])
    upper = jnp.where(even, ring_a[0], ring_b[0])
    rim[0] = jnp.where(column > 0, lower, 0.0)
    rim[1] = jnp.where(column < last, upper, 0.0)


def rim_level(level, rim, index, weights, e_out):
    count = e_out.shape[0] // SUB
    at = slice(level * LANES, (level + 1) * LANES)
    sums = [None] * count
    for face in range(index.shape[0]):
        if inflow_only(face, level):
            continue
        sources = [(1 + s, lambda i, s=s: rim[s, rows_of(i), :]) for s in range(2)]
        values = face_values(face, level, sources, index, count)
        weight = jnp.broadcast_to(weights[face : face + 1, at], (SUB, LANES))
        for i in range(count):
            term = values[i] * weight
            sums[i] = term if sums[i] is None else sums[i] + term
    for i in range(count):
        e_out[rows_of(i), at] = sums[i]


def inflow_weights(level, index, weights, s_out):
    at = slice(level * LANES, (level + 1) * LANES)
    source = iota((LANES, LANES), 0)
    total = None
    for face in range(index.shape[0]):
        hit = index[face : face + 1, at] == source
        term = jnp.where(hit, weights[face : face + 1, at], 0.0)
        total = term if total is None else total + term
    high, low = split(total)
    s_out[:, at] = high
    s_out[:, slice(s_out.shape[1] // 2 + at.start, s_out.shape[1] // 2 + at.stop)] = low


def older_rows(level):
    return sum(max(v - LAG + 1, 0) for v in range(level)) * LANES


def own_weights(level, index, weights, own):
    depth = (level - LAG + 1) * LANES
    if depth <= 0:
        return
    at = slice(level * LANES, (level + 1) * LANES)
    source = iota((depth, LANES), 0) + 3 * LANES
    total = None
    for face in range(index.shape[0]):
        if inflow_only(face, level):
            continue
        hit = index[face : face + 1, at] == source
        term = jnp.where(hit, weights[face : face + 1, at], 0.0)
        total = term if total is None else total + term
    high, low = split(total)
    start = older_rows(level)
    own[start : start + depth, :LANES] = high
    own[start : start + depth, LANES:] = low


def sweep(
    inflow, live, r, w, index, weights, s, own, e, traces_out, pool, ends, narrow, stacked, face_dofs
):
    faces, cells = index.shape
    levels = cells // LANES
    rows = e.shape[0]
    count = rows // SUB
    per_dof = count // face_dofs
    pair = 2 * LANES
    if inflow is not None:
        high, low = split(inflow[...])
        ends[:rows, :] = high
        ends[rows:, :] = low
    for level in range(levels):
        at = slice(level * LANES, (level + 1) * LANES)
        if inflow is not None and level % 2 == 0:
            both = slice(level * LANES, level * LANES + pair)
            main = jnp.dot(ends[...], s[:, both], preferred_element_type=F32)
            rest = jnp.dot(
                ends[:rows, :],
                s[:, slice(cells + both.start, cells + both.stop)],
                preferred_element_type=F32,
            )
            given = e[:, both] + (main[:rows] + (main[rows:] + rest))
        if inflow is None:
            sums = [e[rows_of(i), at] for i in range(count)]
        else:
            half = slice(level % 2 * LANES, (level % 2 + 1) * LANES)
            sums = [given[rows_of(i), half] for i in range(count)]
        oldest = 0
        if own is not None and level >= LAG:
            oldest = level - LAG + 1
            start = older_rows(level)
            got = jnp.dot(
                narrow[:, : oldest * LANES],
                own[start : start + oldest * LANES, :],
                preferred_element_type=F32,
            )
            got = got[:rows, :LANES] + (got[rows:, :LANES] + got[:rows, LANES:])
            sums = [sums[i] + got[rows_of(i), :] for i in range(count)]
        for face in range(faces):
            if inflow_only(face, level) or level == 0:
                continue
            sources = [
                (3 + v, lambda i, v=v: pool[v, rows_of(i), :])
                for v in range(oldest, level)
            ]
            values = face_values(face, level, sources, index, count)
            weight = jnp.broadcast_to(weights[face : face + 1, at], (SUB, LANES))
            for i in range(count):
                sums[i] = sums[i] + values[i] * weight
        spot = at
        for i in range(0, count, 2):
            masked = jnp.concatenate([sums[i], sums[i + 1]], axis=0) * live[:, at]
            high, low = split(masked)
            stacked[i * SUB : (i + 2) * SUB, spot] = high
            stacked[rows + i * SUB : rows + (i + 2) * SUB, spot] = low
        for f in range(face_dofs):
            mix = [
                jnp.broadcast_to(w[face_dofs * f + g : face_dofs * f + g + 1, at], (SUB, LANES))
                for g in range(face_dofs)
            ]
            for k in range(per_dof):
                i = f * per_dof + k
                value = r[rows_of(i), at]
                for g in range(face_dofs):
                    value = value + mix[g] * sums[g * per_dof + k]
                if level < levels - 1:
                    pool[level, rows_of(i), :] = value
                else:
                    traces_out[rows_of(i), :] = value
        if own is not None and level < levels - LAG:
            high, low = split(pool[level])
            narrow[:rows, at] = high
            narrow[rows:, at] = low


def local_group(j, mask, inv, rhs, p_out, wide):
    block = inv.shape[0]
    start = pl.multiple_of(j * LANES, LANES)
    at = pl.ds(start, LANES)
    for a in range(block):
        wide[a * block : (a + 1) * block, :] = inv[a, :, at].astype(F32) * mask[:, at]
    step = block // 2

    def some(part, carry):
        sums = [None] * step
        for b in range(block):
            source = rhs[b, :, at].astype(F32)
            for i in range(step):
                row = (part * step + i) * block + b
                term = wide[pl.ds(row, 1), :] * source
                sums[i] = term if sums[i] is None else sums[i] + term
        for i in range(step):
            p_out[part * step + i, :, at] = sums[i]
        return carry

    lax.fori_loop(0, block // step, some, 0)


def local_plan(flows, groups):
    plan = []
    for f in range(flows):
        turns = [("turn", m) for m in range(1, f if f > 2 else f - 1)]
        late = [("window", m) for m in range(max(f, min(1, flows - 2)), flows - 1)]
        steps = turns + late or [("final", flows - 1)]
        shares = [1] * len(turns) + [3] * len(late) or [1]
        ends = [-(-sum(shares[:k]) * groups // sum(shares)) for k in range(len(steps) + 1)]
        plan.append({step: (ends[k], ends[k + 1]) for k, step in enumerate(steps)})
    return plan


def planned_groups(step, flow, mask, inv, rhs, p_out, wide):
    flows = lax.axis_size(flow)
    plan = local_plan(flows, rhs.shape[2] // LANES)
    if not any(step in own for own in plan):
        return
    position = lax.axis_index(flow)
    first = end = 0
    for f in range(flows):
        low, high = plan[f].get(step, (0, 0))
        first = jnp.where(position == f, low, first)
        end = jnp.where(position == f, high, end)
    lax.fori_loop(
        first, end, lambda j, c: (local_group(j, mask, inv, rhs, p_out, wide), c)[1], 0
    )


def turn(*refs, moment, flow, face_dofs):
    refs = list(refs)
    inflow = refs.pop(0) if moment > 0 else None
    live, r, w, index, weights, e, own = refs[:7]
    s, mask = (refs.pop(7), refs.pop(7)) if moment > 0 else (None, None)
    inv, rhs, _, _, p_out, stacked, traces_out, pool, wide, narrow = refs[7:17]
    ends = refs[17] if moment > 0 else None

    @pl.when(lax.axis_index(flow) == moment)
    def _():
        sweep(
            inflow,
            live,
            r,
            w,
            index,
            weights,
            s,
            own,
            e,
            traces_out,
            pool,
            ends,
            narrow,
            stacked,
            face_dofs,
        )

    planned_groups(("turn", moment), flow, mask, inv, rhs, p_out, wide)


def window(mask, inv, rhs, _, p_out, wide, *, moment, flow):
    planned_groups(("window", moment), flow, mask, inv, rhs, p_out, wide)


def early(mask, inv, rhs, carried, qt, il, _, p, out, wide, done, sem, *, moment, flow):
    planned_groups(("window", moment), flow, mask, inv, rhs, p, wide)

    @pl.when(lax.axis_index(flow) <= moment)
    def _():
        write_solution(carried, qt, p, il, out, done, sem)


def final(mask, inv, rhs, carried, qt, il, _, out_in, p, out, wide, done, sem, *, flow):
    last = lax.axis_size(flow) - 1
    planned_groups(("final", last), flow, mask, inv, rhs, p, wide)

    @pl.when(lax.axis_index(flow) == last)
    def _():
        write_solution(carried, qt, p, il, out, done, sem)


def write_solution(carried, qt, p, il, out, done, sem):
    block, tracers, cells = p.shape
    rows = carried.shape[0] // 2
    face_dofs = rows // tracers
    width = 2 * LANES
    parts = cells // width

    def copy_of(part):
        at = pl.ds(pl.multiple_of(part * width, width), width)
        return pltpu.make_async_copy(done.at[:, :, at], out.at[:, :, at], sem.at[part])

    def moved_to(part):
        cols = pl.ds(pl.multiple_of(part * width, width), width)
        back = jnp.dot(carried[...], qt[:, cols], preferred_element_type=F32)
        return back[:rows] + back[rows:]

    def write(part, moved):
        for k in range(2):
            at = pl.ds(pl.multiple_of(part * width + k * LANES, LANES), LANES)
            half = slice(k * LANES, (k + 1) * LANES)
            for a in range(block):
                value = p[a, :, at]
                for g in range(face_dofs):
                    scale = il[g * block + a : g * block + a + 1, at]
                    value = value + scale * moved[g * tracers : (g + 1) * tracers, half]
                done[a, :, at] = value
        copy_of(part).start()

    def one(part, moved):
        following = moved_to(part + 1)
        write(part, moved)
        return following

    write(parts - 1, lax.fori_loop(0, parts - 1, one, moved_to(0)))
    for part in range(parts):
        copy_of(part).wait()


def swaps(flows, columns, partner):
    pairs = []
    for f in range(flows):
        for c in range(columns):
            to_f, to_c = partner(f, c)
            if not (0 <= to_f < flows and 0 <= to_c < columns):
                to_f, to_c = f, c
            pairs.append((f * columns + c, to_f * columns + to_c))
    return pairs


def rim_partner(first, columns):
    def partner(f, c):
        other = c + 1 if c % 2 == first else c - 1
        return (f, other) if 0 <= other < columns else (f ^ 1, c)

    return partner


def hop_partner(moment):
    def partner(f, c):
        return (2 * moment + 1 - f, c) if f in (moment, moment + 1) else (f, c ^ 1)

    return partner


def shards(
    rhs,
    inverses,
    flux_weights,
    upwind_index,
    sweep_order,
    level_counts,
    boundary_traces,
    trace_map,
    lift_map,
):
    _, _, block, tracers, cells = rhs.shape
    face_dofs = trace_map.shape[0]
    rows = face_dofs * tracers
    flows = lax.axis_size("flow")
    columns = lax.axis_size("cross")
    edges = boundary_traces.reshape(2, rows, LANES)
    axes = ("flow", "cross")
    ring_a = lax.ppermute(edges, axes, swaps(flows, columns, rim_partner(0, columns)))
    ring_b = lax.ppermute(edges, axes, swaps(flows, columns, rim_partner(1, columns)))
    faces = upwind_index.shape[2]
    far = pl.BlockSpec(memory_space=pltpu.HBM)

    ti, il, mix, q, inv, rhs, index, weights, live, p, carried, order = pl.pallas_call(
        load,
        out_shape=(
            pltpu.VMEM((face_dofs * block, cells), F32),
            pltpu.VMEM((face_dofs * block, cells), F32),
            pltpu.VMEM((2 * WROWS, cells), BF16),
            pltpu.VMEM((cells, cells), BF16),
            pltpu.VMEM((block, block, cells), BF16),
            pltpu.VMEM((block, tracers, cells), BF16),
            pltpu.VMEM((faces, cells), jnp.int32),
            pltpu.VMEM((faces, cells), F32),
            pltpu.VMEM((1, cells), F32),
            pltpu.VMEM((block, tracers, cells), F32),
            pltpu.VMEM((2 * rows, cells), BF16),
            pltpu.VMEM((1, cells), jnp.int32),
        ),
        in_specs=[far] * 8,
        out_specs=(VM,) * 12,
        scratch_shapes=[
            pltpu.SMEM((cells // LANES,), jnp.int32),
            pltpu.VMEM((face_dofs, block), F32),
            pltpu.VMEM((face_dofs, block), F32),
            pltpu.SemaphoreType.DMA((8,)),
        ],
        compiler_params=params(12),
        name="load",
    )(
        in_hbm(level_counts[0, 0]),
        in_hbm(inverses[0, 0]),
        in_hbm(rhs[0, 0]),
        in_hbm(sweep_order[0]),
        in_hbm(upwind_index[0, 0]),
        in_hbm(flux_weights[0, 0]),
        in_hbm(trace_map),
        in_hbm(lift_map.T),
    )

    e_shape = pltpu.VMEM((rows, cells), F32)
    rim_shape = pltpu.VMEM((2, rows, LANES), F32)
    p_shape = pltpu.VMEM((block, tracers, cells), F32)
    halves = pltpu.VMEM((2 * rows, cells), BF16)
    sent = pltpu.VMEM((rows, LANES), F32)
    pool = pltpu.VMEM((cells // LANES, rows, LANES), F32)
    wide = pltpu.VMEM((block * block, LANES), F32)
    ends = pltpu.VMEM((2 * rows, LANES), BF16)
    out_shape = pltpu.HBM((block, tracers, cells), F32)
    out_scratch = [wide, p_shape, pltpu.SemaphoreType.DMA((cells // (2 * LANES),))]

    r, w, own = pl.pallas_call(
        products,
        out_shape=[
            pltpu.VMEM((rows, cells), F32),
            pltpu.VMEM((WROWS, cells), F32),
            pltpu.VMEM((max(older_rows(cells // LANES), LANES), 2 * LANES), BF16),
        ],
        in_specs=[VM] * 7,
        out_specs=[VM] * 3,
        scratch_shapes=[pltpu.VMEM((2 * (rows + WROWS), cells), BF16)],
        compiler_params=params(8),
        name="products",
    )(ti, mix, rhs, q, live, index, weights)
    rim_given = [in_vmem(ring_a), in_vmem(ring_b), index, weights]
    e = pl.pallas_call(
        functools.partial(rim_first, axes=axes),
        out_shape=e_shape,
        in_specs=[VM] * 4,
        out_specs=VM,
        scratch_shapes=[rim_shape],
        compiler_params=params(4),
        name="rim_first",
    )(*rim_given)

    s = qt = mask = received = out = None
    for moment in range(flows):
        last = moment == flows - 1
        given = [] if moment == 0 else [in_vmem(received)]
        given += [live, r, w, index, weights, e, own] + ([] if moment == 0 else [s, mask])
        given += [inv, rhs, p, carried]
        made = pl.pallas_call(
            functools.partial(turn, moment=moment, flow="flow", face_dofs=face_dofs),
            out_shape=[p_shape, halves] + ([] if last else [sent]),
            in_specs=[VM] * len(given),
            out_specs=[VM] * (2 if last else 3),
            input_output_aliases={len(given) - 2: 0, len(given) - 1: 1},
            scratch_shapes=([sent] if last else [])
            + [pool, wide, halves]
            + ([] if moment == 0 else [ends]),
            compiler_params=params(4),
            name=f"turn{moment}",
        )(*given)
        p, carried = made[:2]
        if not last:
            received = lax.ppermute(made[2], axes, swaps(flows, columns, hop_partner(moment)))
        if moment == 0:
            e, s, qt, mask = pl.pallas_call(
                functools.partial(rim_rest, axes=axes),
                out_shape=[
                    e_shape,
                    pltpu.VMEM((LANES, 2 * cells), BF16),
                    pltpu.VMEM((cells, cells), BF16),
                    pltpu.VMEM((1, cells), F32),
                ],
                in_specs=[VM] * 7,
                out_specs=[VM] * 4,
                input_output_aliases={6: 0},
                scratch_shapes=[rim_shape],
                compiler_params=params(8),
                name="rim_rest",
            )(*rim_given, order, live, e)
        if moment == 1:
            qt, mask = pl.pallas_call(
                functools.partial(order_second, flow="flow"),
                out_shape=[
                    pltpu.VMEM((cells, cells), BF16),
                    pltpu.VMEM((1, cells), F32),
                ],
                in_specs=[VM] * 4,
                out_specs=[VM] * 2,
                input_output_aliases={2: 0, 3: 1},
                compiler_params=params(4),
                name="order_second",
            )(order, live, qt, mask)
        if moment == flows - 2:
            p, out = pl.pallas_call(
                functools.partial(early, moment=moment, flow="flow"),
                out_shape=[p_shape, out_shape],
                in_specs=[VM] * 7,
                out_specs=[VM, far],
                input_output_aliases={6: 0},
                scratch_shapes=out_scratch,
                compiler_params=params(8),
                name="early",
            )(mask, inv, rhs, carried, qt, il, p)
        elif 0 < moment < flows - 2:
            p = pl.pallas_call(
                functools.partial(window, moment=moment, flow="flow"),
                out_shape=p_shape,
                in_specs=[VM] * 4,
                out_specs=VM,
                input_output_aliases={3: 0},
                scratch_shapes=[wide],
                compiler_params=params(4),
                name=f"window{moment}",
            )(mask, inv, rhs, p)

    if out is None:
        out = jnp.zeros((block, tracers, cells), F32)
    p, out = pl.pallas_call(
        functools.partial(final, flow="flow"),
        out_shape=[p_shape, out_shape],
        in_specs=[VM] * 7 + [far],
        out_specs=[VM, far],
        input_output_aliases={6: 0, 7: 1},
        scratch_shapes=out_scratch,
        compiler_params=params(8),
        name="final",
    )(mask, inv, rhs, carried, qt, il, p, out)
    return out[None, None]


def solution(mesh):
    placed = (
        P("flow", "cross", None, None, None),
        P("flow", "cross", None, None, None),
        P("flow", "cross", None, None),
        P("flow", "cross", None, None),
        P("flow", "cross", None),
        P("flow", "cross", None),
        P("flow", "cross", None, None, None),
        P(),
        P(),
    )
    return jax.shard_map(
        shards,
        mesh=mesh,
        in_specs=placed,
        out_specs=P("flow", "cross", None, None, None),
        check_vma=False,
    )
```
